32 devices in a mesh: chan: 8 (over z, y), grp: 4 (over x, core).
Axes of the slice: x: 2, y: 2, z: 4, core: 2. Of those that a mesh axis runs over, the one named last changes fastest.
Arguments:
- record: bfloat16 [6400, 512], P('chan'), may hold values from -6 to 6
- group_lengths: int32 [4, 16], replicated, may hold values from 1 to 384, 512 in all within a row
- source_pick: int32 [4, 16], replicated, may hold values from 0 to 4095
Outputs:
- correlation: float32 [4, 512, 128], P(None, ('chan', 'grp'))
The draws below stay inside these ranges and needn't reach their ends.
Inputs may be any that keep to these rules, and one draw needn't show every extreme that they name: `group_lengths`: each row sums to 512, and its largest entry is 384.
All inputs are finite; a program needn't handle non-finite values.
Results may differ from the reference program's by a relative error of at most 0.02.
Values may be sent and summed in bfloat16 or wider, within the bound.
A program may use at most 64 MiB of HBM per device.

```python
import math
import jax
import jax.numpy as jnp
import numpy as np
from jax import lax

CH_DEV = 16
SEG = 32
SAMP = 200
LAGS = 128
STEPS = 4
GROUPS = 16
BINS = 101
TIME = 6400
NCH = 512
N_CHAN = 8
N_GRP = 4


def touch_ends(entries, rng, least, largest):
    extent = entries.shape
    spot = [jax.random.randint(jax.random.fold_in(rng, axis), (), 0, extent[axis]) for axis in range(len(extent))]
    entries = entries.at[tuple(spot)].set(least)
    longest = extent.index(max(extent))
    spot[longest] = (spot[longest] + 1) % extent[longest]
    return entries.at[tuple(spot)].set(largest)


def block_levels(key, dims, pieces, low, top_value):
    def one(axis_at, blocks):
        heights = jax.random.uniform(jax.random.fold_in(jax.random.fold_in(key, 6), axis_at), (blocks,), jnp.float32, low / len(pieces), top_value / len(pieces))
        return jnp.repeat(jnp.exp(heights), dims[axis_at] // blocks).reshape((-1,) + (1,) * (len(dims) - axis_at - 1))

    loudness = one(*pieces[0])
    for cut in pieces[1:]:
        loudness = loudness * one(*cut)
    return loudness


def profile(count, total, limit, slope):
    portions = [(1 << 20) // math.isqrt(rank ** slope) + 1 for rank in range(2, count + 1)]
    rest, counts = total - limit - (count - 1), [1] * (count - 1)
    while rest > 0:
        free = [i for i in range(count - 1) if counts[i] < limit]
        whole, remaining = sum([portions[i] for i in free]), rest
        for i in free:
            extra = min(limit - counts[i], max(1, remaining * portions[i] // whole), rest)
            counts[i] = counts[i] + extra
            rest = rest - extra
    return np.array([limit] + counts)


def uneven(rng, count, total, reach, slope):
    if count == 2:
        one = jax.random.randint(rng, (), max(1, total - reach), min(reach, total - 1) + 1)
        return jnp.stack([one, total - one])
    sizes = jnp.asarray(profile(count, total, reach, slope), jnp.int32)
    twos = (count - 1) // 2
    giver, sink = sizes[1:1 + 2 * twos:2], sizes[2:2 + 2 * twos:2]
    margin = jnp.minimum(giver - 1, reach - sink)
    passed = jax.random.randint(jax.random.fold_in(rng, 1), (twos,), 0, 1 << 20) % (margin + 1)
    sizes = sizes.at[1:1 + 2 * twos:2].set(giver - passed).at[2:2 + 2 * twos:2].set(sink + passed)
    return sizes[jax.random.permutation(jax.random.fold_in(rng, 2), count)]


def centred(rng, shape, spread, reach, pieces=(), held_as=jnp.bfloat16):
    drawn = spread * jax.random.normal(rng, shape, jnp.float32)
    if pieces:
        drawn = drawn * block_levels(rng, shape, pieces, -0.22, 0.18)
    return jnp.clip(drawn, -reach, reach).astype(held_as)


def setup_inputs(seed: int = 0) -> dict:
    splits = jax.random.split(jax.random.key(seed), 4)
    record = centred(splits[0], (TIME, NCH), 1.0, 6.0, ((0, 8),))
    group_lengths = jax.vmap(lambda own: uneven(own, GROUPS, NCH, 3 * NCH // 4, 2))(jax.random.split(splits[1], STEPS)).reshape((STEPS, GROUPS)).astype(jnp.int32)
    source_pick = touch_ends(jax.random.randint(splits[2], (STEPS, GROUPS), 0, 4096), jax.random.fold_in(splits[2], 1), 0, 4095).astype(jnp.int32)
    return dict(record=record, group_lengths=group_lengths, source_pick=source_pick)


def dft_table(samples_count, bins_count):
    samples = jnp.arange(samples_count, dtype=jnp.int32)[:, None]
    freqs = jnp.arange(2 * bins_count, dtype=jnp.int32)[None, :]
    folded = jnp.where(freqs < bins_count, freqs, freqs - bins_count)
    phase = (samples * folded % samples_count).astype(jnp.float32) * (2.0 * math.pi / samples_count)
    return jnp.where(freqs < bins_count, jnp.cos(phase), -jnp.sin(phase)).astype(jnp.bfloat16)

def lag_table(samples_count, bins_count, lag_count):
    freq_rows = jnp.arange(2 * bins_count, dtype=jnp.int32)[:, None]
    lag_cols = jnp.arange(lag_count, dtype=jnp.int32)[None, :] - lag_count // 2
    folded = jnp.where(freq_rows < bins_count, freq_rows, freq_rows - bins_count)
    phase = (folded * lag_cols % samples_count).astype(jnp.float32) * (2.0 * math.pi / samples_count)
    weights = jnp.where((folded == 0) | (folded == samples_count // 2), 1.0, 2.0).astype(jnp.float32)
    return weights * jnp.where(freq_rows < bins_count, jnp.cos(phase), -jnp.sin(phase))

def whiten(strain):
    values = strain.astype(jnp.float32).reshape(SEG, SAMP, strain.shape[1])
    means = lax.optimization_barrier(jnp.mean(values, axis=1, keepdims=True))
    centered = values - means
    mean_square = lax.optimization_barrier(jnp.mean(centered * centered, axis=1, keepdims=True))
    return (centered / jnp.sqrt(mean_square + 1e-06)).astype(jnp.bfloat16)

def reference(record, group_lengths, source_pick):
    block_size = CH_DEV * N_CHAN
    block_count = N_GRP
    padded = jnp.pad(record, ((0, 0), (1, 1)))
    table = dft_table(SAMP, BINS)

    def spectra_of(block_index):
        window = lax.dynamic_slice_in_dim(padded, block_index * block_size, block_size + 2, 1).astype(jnp.float32)
        strain = ((window[:, 2:] - window[:, :-2]) * 0.5).astype(jnp.bfloat16)
        whitened = whiten(strain)
        return jnp.einsum('snc,nk->skc', whitened.astype(jnp.float32), table.astype(jnp.float32), precision=lax.Precision.HIGHEST).astype(jnp.bfloat16)
    spectra = lax.map(spectra_of, jnp.arange(block_count, dtype=jnp.int32))
    finish = jnp.cumsum(group_lengths, axis=1).astype(jnp.int32)
    starts = (finish - group_lengths).astype(jnp.int32)
    source = (starts + group_lengths * source_pick // 65536).astype(jnp.int32)
    source_spec = spectra[source // block_size, :, :, source % block_size]
    lagt = lag_table(SAMP, BINS, LAGS)

    def correlate(block_index):
        receiver = spectra[block_index].astype(jnp.float32)
        channels = block_index * block_size + jnp.arange(block_size, dtype=jnp.int32)
        rec_real = receiver[:, :BINS]
        rec_imag = receiver[:, BINS:]
        traces = []
        for step_index in range(STEPS):
            source_now = source_spec[step_index].astype(jnp.float32)
            src_real = source_now[..., :BINS]
            src_imag = source_now[..., BINS:]
            real_all = jnp.einsum('ksf,sfc->fkc', src_real, rec_real, precision=lax.Precision.HIGHEST) + jnp.einsum('ksf,sfc->fkc', src_imag, rec_imag, precision=lax.Precision.HIGHEST)
            imag_all = jnp.einsum('ksf,sfc->fkc', src_real, rec_imag, precision=lax.Precision.HIGHEST) - jnp.einsum('ksf,sfc->fkc', src_imag, rec_real, precision=lax.Precision.HIGHEST)
            members = ((channels[None, :] >= starts[step_index][:, None]) & (channels[None, :] < finish[step_index][:, None])).astype(jnp.float32)
            cross_real = lax.optimization_barrier(jnp.sum(real_all * members[None], axis=1))
            cross_imag = lax.optimization_barrier(jnp.sum(imag_all * members[None], axis=1))
            cross_spectrum = jnp.concatenate([cross_real, cross_imag], axis=0)
            lagged = jnp.dot(cross_spectrum.T, lagt, precision=lax.Precision.HIGHEST, preferred_element_type=jnp.float32)
            inverse_rms = 1.0 / jnp.sqrt(lax.optimization_barrier(jnp.mean(lagged * lagged, axis=1, keepdims=True)) + 1e-06)
            traces.append(lagged * inverse_rms)
        return jnp.stack(traces)
    result = lax.map(correlate, jnp.arange(block_count, dtype=jnp.int32))
    return jnp.transpose(result, (1, 0, 2, 3)).reshape(STEPS, block_count * block_size, LAGS)
```

```python
import functools
import math

import jax
import jax.numpy as jnp
import numpy as np
from jax import lax
from jax.experimental import pallas as pl
from jax.experimental.pallas import tpu as pltpu
from jax.sharding import PartitionSpec as P

CH_DEV = 16
SEG = 32
SAMP = 200
LAGS = 128
STEPS = 4
GROUPS = 16
BINS = 101


def extended(array, sides, width):
    for axis, dim in sides:
        count, length = (lax.axis_size(axis), array.shape[dim])
        up = [(i, (i + 1) % count) for i in range(count - 1)]
        down = [(j, i) for i, j in up]
        last = lax.slice_in_dim(array, length - width, length, axis=dim)
        first = lax.slice_in_dim(array, 0, width, axis=dim)
        before = lax.ppermute(last, axis, up)
        after = lax.ppermute(first, axis, down)
        array = jnp.concatenate([before, array, after], axis=dim)
    return array


def dft_table(samples_count, bins_count):
    samples = jnp.arange(samples_count, dtype=jnp.int32)[:, None]
    freqs = jnp.arange(2 * bins_count, dtype=jnp.int32)[None, :]
    folded = jnp.where(freqs < bins_count, freqs, freqs - bins_count)
    phase = (samples * folded % samples_count).astype(jnp.float32) * (2.0 * math.pi / samples_count)
    return jnp.where(freqs < bins_count, jnp.cos(phase), -jnp.sin(phase)).astype(jnp.bfloat16)


def lag_table(samples_count, bins_count, lag_count):
    freq_rows = jnp.arange(2 * bins_count, dtype=jnp.int32)[:, None]
    lag_cols = jnp.arange(lag_count, dtype=jnp.int32)[None, :] - lag_count // 2
    folded = jnp.where(freq_rows < bins_count, freq_rows, freq_rows - bins_count)
    phase = (folded * lag_cols % samples_count).astype(jnp.float32) * (
        2.0 * math.pi / samples_count
    )
    weights = jnp.where((folded == 0) | (folded == samples_count // 2), 1.0, 2.0).astype(
        jnp.float32
    )
    return weights * jnp.where(freq_rows < bins_count, jnp.cos(phase), -jnp.sin(phase))


def whiten(strain):
    values = strain.astype(jnp.float32).reshape(SEG, SAMP, strain.shape[1])
    means = jnp.mean(values, axis=1, keepdims=True)
    centered = values - means
    mean_square = jnp.mean(centered * centered, axis=1, keepdims=True)
    return (centered / jnp.sqrt(mean_square + 1e-06)).astype(jnp.bfloat16)


def spectral(left, right):
    return jnp.einsum("ksf,sfc->fkc", left, right, preferred_element_type=jnp.float32)


def shards(record, group_lengths, source_pick):
    group_rank = lax.axis_index("grp")
    columns = lax.all_to_all(record, "chan", split_axis=1, concat_axis=0, tiled=True)
    mine = lax.dynamic_slice_in_dim(columns, group_rank * CH_DEV, CH_DEV, 1)
    padded = extended(mine, ((("chan", "grp"), 1),), 1)
    window = padded.astype(jnp.float32)
    strain = ((window[:, 2:] - window[:, :-2]) * 0.5).astype(jnp.bfloat16)
    whitened = whiten(strain)
    spectra = jnp.einsum(
        "snc,nk->skc", whitened, dft_table(SAMP, BINS), preferred_element_type=jnp.float32
    ).astype(jnp.bfloat16)
    first_channel = lax.axis_index(("chan", "grp")) * CH_DEV
    order = jnp.arange(GROUPS, dtype=jnp.int32)
    up_to = order[None, :] <= order[:, None]
    finish = jnp.sum(jnp.where(up_to[None], group_lengths[:, None, :], 0), axis=2)
    starts = finish - group_lengths
    source = starts + group_lengths * source_pick // 65536
    channels = first_channel + jnp.arange(CH_DEV, dtype=jnp.int32)
    owned = (source.reshape(1, -1) == channels[:, None]).astype(jnp.bfloat16)
    partial_table = jnp.einsum("skc,cj->skj", spectra, owned, preferred_element_type=jnp.float32)
    summed = lax.psum(partial_table, ("chan", "grp"))
    source_spec = jnp.transpose(summed.astype(jnp.bfloat16), (2, 0, 1))
    source_spec = source_spec.reshape(STEPS, GROUPS, SEG, 2 * BINS)
    lagt = lag_table(SAMP, BINS, LAGS)
    rec_real = spectra[:, :BINS]
    rec_imag = spectra[:, BINS:]
    traces = []
    for step_index in range(STEPS):
        source_now = source_spec[step_index]
        src_real = source_now[..., :BINS]
        src_imag = source_now[..., BINS:]
        real_all = spectral(src_real, rec_real) + spectral(src_imag, rec_imag)
        imag_all = spectral(src_real, rec_imag) - spectral(src_imag, rec_real)
        members = (
            (channels[None, :] >= starts[step_index][:, None])
            & (channels[None, :] < finish[step_index][:, None])
        ).astype(jnp.float32)
        cross_real = jnp.sum(real_all * members[None], axis=1)
        cross_imag = jnp.sum(imag_all * members[None], axis=1)
        cross_spectrum = jnp.concatenate([cross_real, cross_imag], axis=0)
        lagged = jnp.dot(
            cross_spectrum.T,
            lagt,
            precision=lax.Precision.HIGHEST,
            preferred_element_type=jnp.float32,
        )
        inverse_rms = 1.0 / jnp.sqrt(jnp.mean(lagged * lagged, axis=1, keepdims=True) + 1e-06)
        traces.append(lagged * inverse_rms)
    return jnp.stack(traces)


HALF = 104
SRC = 128


def half_rows(real, imag):
    padded = np.zeros((2, HALF) + real.shape[1:], np.float32)
    padded[0, :BINS] = real
    padded[1, :BINS] = imag
    return padded.reshape((2 * HALF,) + real.shape[1:])


def dft_rows():
    turns = np.arange(BINS)[:, None] * np.arange(SAMP)[None, :] % SAMP
    phase = turns * (2.0 * math.pi / SAMP)
    return half_rows(np.cos(phase), -np.sin(phase))


def lag_rows():
    freqs = np.arange(BINS)[:, None]
    phase = freqs * (np.arange(LAGS)[None, :] - LAGS // 2) % SAMP * (2.0 * math.pi / SAMP)
    weights = np.where((freqs == 0) | (freqs == SAMP // 2), 1.0, 2.0)
    return half_rows(weights * np.cos(phase), -weights * np.sin(phase))


def partial_kernel(
    n_chan,
    n_grp,
    rec_hbm,
    lengths_hbm,
    pick_hbm,
    dft_hbm,
    lag_hbm,
    out_ref,
    lengths_ref,
    pick_ref,
    rec_buf,
    dft_ref,
    lag_ref,
    send_buf,
    recv_buf,
    load_sems,
    send_sems,
    recv_sems,
):
    rows, n_ch = rec_buf.shape
    n_recv = n_chan * CH_DEV
    me, group = lax.axis_index("chan"), lax.axis_index("grp")
    loads = [
        pltpu.make_async_copy(src, dst, load_sems.at[i])
        for i, (src, dst) in enumerate(
            [
                (lengths_hbm, lengths_ref),
                (pick_hbm, pick_ref),
                (rec_hbm, rec_buf),
                (dft_hbm, dft_ref),
                (lag_hbm, lag_ref),
            ]
        )
    ]
    for load in loads:
        load.start()
    small, large = loads[:2], loads[2:]
    barrier = pltpu.get_barrier_semaphore()
    hops = sorted(range(1, n_chan), key=lambda hop: min(hop, n_chan - hop))
    peers = [lax.rem(me + hop, n_chan) for hop in hops]
    for peer in peers:
        pl.semaphore_signal(
            barrier,
            inc=1,
            device_id=(peer, group),
            device_id_type=pl.DeviceIdType.MESH,
        )

    for copy in small:
        copy.wait()
    reps = SRC // GROUPS
    line = lax.broadcasted_iota(jnp.int32, (STEPS, SRC), 1)
    own_step = lax.broadcasted_iota(jnp.int32, (STEPS, SRC), 0) == line // GROUPS

    def in_line(table):
        tiled = jnp.concatenate([table.astype(jnp.float32)] * reps, axis=1)
        return jnp.sum(jnp.where(own_step, tiled, 0.0), axis=0, keepdims=True)

    lengths = in_line(lengths_ref[...])
    down = lax.broadcasted_iota(jnp.int32, (SRC, SRC), 0)
    along = lax.broadcasted_iota(jnp.int32, (SRC, SRC), 1)
    lengths_down = jnp.sum(jnp.where(down == along, lengths, 0.0), axis=1, keepdims=True)
    same = down // GROUPS == along // GROUPS
    starts = jnp.sum(jnp.where(same & (down < along), lengths_down, 0.0), axis=0, keepdims=True)
    starts_down = jnp.sum(jnp.where(same & (along < down), lengths, 0.0), axis=1, keepdims=True)
    starts_down = starts_down.astype(jnp.int32)
    finish_down = starts_down + lengths_down.astype(jnp.int32)
    product = lengths.astype(jnp.int32) * in_line(pick_ref[...]).astype(jnp.int32)
    source = starts.astype(jnp.int32) + lax.shift_right_logical(product, 16)

    place = lax.broadcasted_iota(jnp.int32, (1, n_recv), 1)
    receivers = (place // CH_DEV) * (n_grp * CH_DEV) + group * CH_DEV + place % CH_DEV
    columns = jnp.concatenate([receivers, source], axis=1)
    apart = lax.broadcasted_iota(jnp.int32, (n_ch, n_recv + SRC), 0) - columns
    gauge = jnp.where(apart == 1, 0.5, jnp.where(apart == -1, -0.5, 0.0)).astype(jnp.bfloat16)
    slot = lax.broadcasted_iota(jnp.int32, (SRC, n_recv), 0) // GROUPS
    member = (starts_down <= receivers) & (receivers < finish_down)
    spread = jnp.concatenate(
        [jnp.where(member & (slot == j), 1.0, 0.0) for j in range(STEPS)], axis=1
    ).astype(jnp.bfloat16)

    for load in large:
        load.wait()
    strain = jnp.dot(rec_buf[...], gauge, preferred_element_type=jnp.float32)
    held = []
    for seg in range(rows // SAMP):
        values = strain[seg * SAMP : (seg + 1) * SAMP].astype(jnp.bfloat16).astype(jnp.float32)
        centered = values - jnp.sum(values, axis=0, keepdims=True) * (1.0 / SAMP)
        mean_square = jnp.sum(centered * centered, axis=0, keepdims=True) * (1.0 / SAMP)
        whitened = (centered * lax.rsqrt(mean_square + 1e-06)).astype(jnp.bfloat16)
        spec = jnp.dot(dft_ref[...], whitened, preferred_element_type=jnp.float32)
        spec = spec.astype(jnp.bfloat16)
        receiver = spec[:, :n_recv].astype(jnp.float32)
        source = jnp.dot(spec[:, n_recv:], spread, preferred_element_type=jnp.float32)
        held.append((receiver, source))
    for j in range(STEPS):
        real, imag = 0.0, 0.0
        for receiver, source in held:
            rec_real, rec_imag = receiver[:HALF], receiver[HALF:]
            src_real = source[:HALF, j * n_recv : (j + 1) * n_recv]
            src_imag = source[HALF:, j * n_recv : (j + 1) * n_recv]
            real += src_real * rec_real + src_imag * rec_imag
            imag += src_real * rec_imag - src_imag * rec_real
        cross = jnp.concatenate([real, imag], axis=0).astype(jnp.bfloat16)
        lagged = jnp.dot(lag_ref[...], cross, preferred_element_type=jnp.float32)
        lagged = lagged.astype(jnp.bfloat16).T
        send_buf[:, j] = lagged.reshape(n_chan, CH_DEV, LAGS)

    pl.semaphore_wait(barrier, n_chan - 1)
    copies = []
    for k, peer in enumerate(peers):
        copy = pltpu.make_async_remote_copy(
            src_ref=send_buf.at[peer],
            dst_ref=recv_buf.at[k],
            send_sem=send_sems.at[k],
            recv_sem=recv_sems.at[k],
            device_id=(peer, group),
            device_id_type=pl.DeviceIdType.MESH,
        )
        copy.start()
        copies.append(copy)
    total = send_buf[me].astype(jnp.float32)
    for k, copy in enumerate(copies):
        copy.wait_recv()
        total += recv_buf[k].astype(jnp.float32)
    mean_square = jnp.sum(total * total, axis=-1, keepdims=True) * (1.0 / LAGS)
    out_ref[...] = total * lax.rsqrt(mean_square + 1e-06)
    for copy in copies:
        copy.wait_send()


def segment_shards(n_chan, n_grp, record, group_lengths, source_pick):
    rows, n_ch = record.shape
    dft = jnp.asarray(dft_rows(), jnp.bfloat16)
    lag = jnp.asarray(lag_rows().T, jnp.bfloat16)
    operands = (record, group_lengths, source_pick, dft, lag)
    block = (STEPS, CH_DEV, LAGS)
    return pl.pallas_call(
        functools.partial(partial_kernel, n_chan, n_grp),
        out_shape=jax.ShapeDtypeStruct(block, jnp.float32),
        in_specs=[pl.BlockSpec(memory_space=pltpu.HBM)] * 5,
        out_specs=pl.BlockSpec(memory_space=pltpu.VMEM),
        scratch_shapes=[
            pltpu.VMEM((STEPS, GROUPS), jnp.int32),
            pltpu.VMEM((STEPS, GROUPS), jnp.int32),
            pltpu.VMEM((rows, n_ch), jnp.bfloat16),
            pltpu.VMEM(dft.shape, jnp.bfloat16),
            pltpu.VMEM(lag.shape, jnp.bfloat16),
            pltpu.VMEM((n_chan,) + block, jnp.bfloat16),
            pltpu.VMEM((n_chan - 1,) + block, jnp.bfloat16),
            pltpu.SemaphoreType.DMA((5,)),
            pltpu.SemaphoreType.DMA((n_chan - 1,)),
            pltpu.SemaphoreType.DMA((n_chan - 1,)),
        ],
        compiler_params=pltpu.CompilerParams(
            collective_id=0, has_side_effects=True, vmem_limit_bytes=32 * 1024 * 1024
        ),
    )(*(pltpu.with_memory_space_constraint(x, pltpu.HBM) for x in operands))


def solution(mesh):
    n_chan, n_grp = mesh.shape["chan"], mesh.shape["grp"]

    def local(record, group_lengths, source_pick):
        rows = record.shape[0]
        if rows % SAMP == 0 and n_chan > 1 and n_chan * CH_DEV % 128 == 0:
            return segment_shards(n_chan, n_grp, record, group_lengths, source_pick)
        return shards(record, group_lengths, source_pick)

    return jax.shard_map(
        local,
        mesh=mesh,
        in_specs=(P("chan", None), P(), P()),
        out_specs=P(None, ("chan", "grp"), None),
        check_vma=False,
    )
```

```python
import functools
import math

import jax
import jax.numpy as jnp
import numpy as np
from jax import lax
from jax.experimental import pallas as pl
from jax.experimental.pallas import tpu as pltpu
from jax.sharding import PartitionSpec as P

CH_DEV = 16
SEG = 32
SAMP = 200
LAGS = 128
STEPS = 4
GROUPS = 16
BINS = 101


def extended(array, sides, width):
    for axis, dim in sides:
        count, length = (lax.axis_size(axis), array.shape[dim])
        up = [(i, (i + 1) % count) for i in range(count - 1)]
        down = [(j, i) for i, j in up]
        last = lax.slice_in_dim(array, length - width, length, axis=dim)
        first = lax.slice_in_dim(array, 0, width, axis=dim)
        before = lax.ppermute(last, axis, up)
        after = lax.ppermute(first, axis, down)
        array = jnp.concatenate([before, array, after], axis=dim)
    return array


def dft_table(samples_count, bins_count):
    samples = jnp.arange(samples_count, dtype=jnp.int32)[:, None]
    freqs = jnp.arange(2 * bins_count, dtype=jnp.int32)[None, :]
    folded = jnp.where(freqs < bins_count, freqs, freqs - bins_count)
    phase = (samples * folded % samples_count).astype(jnp.float32) * (2.0 * math.pi / samples_count)
    return jnp.where(freqs < bins_count, jnp.cos(phase), -jnp.sin(phase)).astype(jnp.bfloat16)


def lag_table(samples_count, bins_count, lag_count):
    freq_rows = jnp.arange(2 * bins_count, dtype=jnp.int32)[:, None]
    lag_cols = jnp.arange(lag_count, dtype=jnp.int32)[None, :] - lag_count // 2
    folded = jnp.where(freq_rows < bins_count, freq_rows, freq_rows - bins_count)
    phase = (folded * lag_cols % samples_count).astype(jnp.float32) * (
        2.0 * math.pi / samples_count
    )
    weights = jnp.where((folded == 0) | (folded == samples_count // 2), 1.0, 2.0).astype(
        jnp.float32
    )
    return weights * jnp.where(freq_rows < bins_count, jnp.cos(phase), -jnp.sin(phase))


def whiten(strain):
    values = strain.astype(jnp.float32).reshape(SEG, SAMP, strain.shape[1])
    means = jnp.mean(values, axis=1, keepdims=True)
    centered = values - means
    mean_square = jnp.mean(centered * centered, axis=1, keepdims=True)
    return (centered / jnp.sqrt(mean_square + 1e-06)).astype(jnp.bfloat16)


def spectral(left, right):
    return jnp.einsum("ksf,sfc->fkc", left, right, preferred_element_type=jnp.float32)


def shards(record, group_lengths, source_pick):
    group_rank = lax.axis_index("grp")
    columns = lax.all_to_all(record, "chan", split_axis=1, concat_axis=0, tiled=True)
    mine = lax.dynamic_slice_in_dim(columns, group_rank * CH_DEV, CH_DEV, 1)
    padded = extended(mine, ((("chan", "grp"), 1),), 1)
    window = padded.astype(jnp.float32)
    strain = ((window[:, 2:] - window[:, :-2]) * 0.5).astype(jnp.bfloat16)
    whitened = whiten(strain)
    spectra = jnp.einsum(
        "snc,nk->skc", whitened, dft_table(SAMP, BINS), preferred_element_type=jnp.float32
    ).astype(jnp.bfloat16)
    first_channel = lax.axis_index(("chan", "grp")) * CH_DEV
    order = jnp.arange(GROUPS, dtype=jnp.int32)
    up_to = order[None, :] <= order[:, None]
    finish = jnp.sum(jnp.where(up_to[None], group_lengths[:, None, :], 0), axis=2)
    starts = finish - group_lengths
    source = starts + group_lengths * source_pick // 65536
    channels = first_channel + jnp.arange(CH_DEV, dtype=jnp.int32)
    owned = (source.reshape(1, -1) == channels[:, None]).astype(jnp.bfloat16)
    partial_table = jnp.einsum("skc,cj->skj", spectra, owned, preferred_element_type=jnp.float32)
    summed = lax.psum(partial_table, ("chan", "grp"))
    source_spec = jnp.transpose(summed.astype(jnp.bfloat16), (2, 0, 1))
    source_spec = source_spec.reshape(STEPS, GROUPS, SEG, 2 * BINS)
    lagt = lag_table(SAMP, BINS, LAGS)
    rec_real = spectra[:, :BINS]
    rec_imag = spectra[:, BINS:]
    traces = []
    for step_index in range(STEPS):
        source_now = source_spec[step_index]
        src_real = source_now[..., :BINS]
        src_imag = source_now[..., BINS:]
        real_all = spectral(src_real, rec_real) + spectral(src_imag, rec_imag)
        imag_all = spectral(src_real, rec_imag) - spectral(src_imag, rec_real)
        members = (
            (channels[None, :] >= starts[step_index][:, None])
            & (channels[None, :] < finish[step_index][:, None])
        ).astype(jnp.float32)
        cross_real = jnp.sum(real_all * members[None], axis=1)
        cross_imag = jnp.sum(imag_all * members[None], axis=1)
        cross_spectrum = jnp.concatenate([cross_real, cross_imag], axis=0)
        lagged = jnp.dot(
            cross_spectrum.T,
            lagt,
            precision=lax.Precision.HIGHEST,
            preferred_element_type=jnp.float32,
        )
        inverse_rms = 1.0 / jnp.sqrt(jnp.mean(lagged * lagged, axis=1, keepdims=True) + 1e-06)
        traces.append(lagged * inverse_rms)
    return jnp.stack(traces)


HALF = 104
SRC = 128


def half_rows(real, imag):
    padded = np.zeros((2, HALF) + real.shape[1:], np.float32)
    padded[0, :BINS] = real
    padded[1, :BINS] = imag
    return padded.reshape((2 * HALF,) + real.shape[1:])


def dft_rows():
    turns = np.arange(BINS)[:, None] * np.arange(SAMP)[None, :] % SAMP
    phase = turns * (2.0 * math.pi / SAMP)
    return half_rows(np.cos(phase), -np.sin(phase))


def lag_rows():
    freqs = np.arange(BINS)[:, None]
    phase = freqs * (np.arange(LAGS)[None, :] - LAGS // 2) % SAMP * (2.0 * math.pi / SAMP)
    weights = np.where((freqs == 0) | (freqs == SAMP // 2), 1.0, 2.0)
    return half_rows(weights * np.cos(phase), -weights * np.sin(phase))


def partial_kernel(
    n_chan,
    n_grp,
    rec_hbm,
    lengths_hbm,
    pick_hbm,
    dft_hbm,
    lag_hbm,
    out_ref,
    lengths_ref,
    pick_ref,
    rec_buf,
    dft_ref,
    lag_ref,
    send_buf,
    recv_buf,
    load_sems,
    send_sems,
    recv_sems,
):
    rows, n_ch = rec_buf.shape
    n_recv = n_chan * CH_DEV
    half = n_chan // 2
    me, group = lax.axis_index("chan"), lax.axis_index("grp")
    pair, side = group // 2, group % 2
    first = (1 - side) * half
    want = jnp.where(me < half, 1, 0)
    keeps = side == want
    source_grp = pair * 2 + want

    def target(slot):
        return (first + slot // 2, pair * 2 + slot % 2)

    loads = [
        pltpu.make_async_copy(src, dst, load_sems.at[i])
        for i, (src, dst) in enumerate(
            [
                (lengths_hbm, lengths_ref),
                (pick_hbm, pick_ref),
                (rec_hbm, rec_buf),
                (dft_hbm, dft_ref),
                (lag_hbm, lag_ref),
            ]
        )
    ]
    for load in loads:
        load.start()
    small, large = loads[:2], loads[2:]
    barrier = pltpu.get_barrier_semaphore()

    def greet(chan):
        pl.semaphore_signal(
            barrier,
            inc=1,
            device_id=(chan, source_grp),
            device_id_type=pl.DeviceIdType.MESH,
        )

    for hop in range(1, n_chan):
        greet(lax.rem(me + hop, n_chan))
    pl.when(jnp.logical_not(keeps))(lambda: greet(me))

    for copy in small:
        copy.wait()
    reps = SRC // GROUPS
    line = lax.broadcasted_iota(jnp.int32, (STEPS, SRC), 1)
    own_step = lax.broadcasted_iota(jnp.int32, (STEPS, SRC), 0) == line // GROUPS

    def in_line(table):
        tiled = jnp.concatenate([table.astype(jnp.float32)] * reps, axis=1)
        return jnp.sum(jnp.where(own_step, tiled, 0.0), axis=0, keepdims=True)

    lengths = in_line(lengths_ref[...])
    down = lax.broadcasted_iota(jnp.int32, (SRC, SRC), 0)
    along = lax.broadcasted_iota(jnp.int32, (SRC, SRC), 1)
    lengths_down = jnp.sum(jnp.where(down == along, lengths, 0.0), axis=1, keepdims=True)
    same = down // GROUPS == along // GROUPS
    starts = jnp.sum(jnp.where(same & (down < along), lengths_down, 0.0), axis=0, keepdims=True)
    starts_down = jnp.sum(jnp.where(same & (along < down), lengths, 0.0), axis=1, keepdims=True)
    starts_down = starts_down.astype(jnp.int32)
    finish_down = starts_down + lengths_down.astype(jnp.int32)
    product = lengths.astype(jnp.int32) * in_line(pick_ref[...]).astype(jnp.int32)
    source = starts.astype(jnp.int32) + lax.shift_right_logical(product, 16)

    place = lax.broadcasted_iota(jnp.int32, (1, n_recv), 1)
    slot_chan, slot_grp = target(place // CH_DEV)
    receivers = (slot_chan * n_grp + slot_grp) * CH_DEV + place % CH_DEV
    columns = jnp.concatenate([receivers, source], axis=1)
    apart = lax.broadcasted_iota(jnp.int32, (n_ch, n_recv + SRC), 0) - columns
    gauge = jnp.where(apart == 1, 0.5, jnp.where(apart == -1, -0.5, 0.0)).astype(jnp.bfloat16)
    slot = lax.broadcasted_iota(jnp.int32, (SRC, n_recv), 0) // GROUPS
    member = (starts_down <= receivers) & (receivers < finish_down)
    spread = jnp.concatenate(
        [jnp.where(member & (slot == j), 1.0, 0.0) for j in range(STEPS)], axis=1
    ).astype(jnp.bfloat16)

    for load in large:
        load.wait()
    strain = jnp.dot(rec_buf[...], gauge, preferred_element_type=jnp.float32)
    held = []
    for seg in range(rows // SAMP):
        values = strain[seg * SAMP : (seg + 1) * SAMP].astype(jnp.bfloat16).astype(jnp.float32)
        centered = values - jnp.sum(values, axis=0, keepdims=True) * (1.0 / SAMP)
        mean_square = jnp.sum(centered * centered, axis=0, keepdims=True) * (1.0 / SAMP)
        whitened = (centered * lax.rsqrt(mean_square + 1e-06)).astype(jnp.bfloat16)
        spec = jnp.dot(dft_ref[...], whitened, preferred_element_type=jnp.float32)
        spec = spec.astype(jnp.bfloat16)
        receiver = spec[:, :n_recv].astype(jnp.float32)
        source = jnp.dot(spec[:, n_recv:], spread, preferred_element_type=jnp.float32)
        held.append((receiver, source))
    for j in range(STEPS):
        real, imag = 0.0, 0.0
        for receiver, source in held:
            rec_real, rec_imag = receiver[:HALF], receiver[HALF:]
            src_real = source[:HALF, j * n_recv : (j + 1) * n_recv]
            src_imag = source[HALF:, j * n_recv : (j + 1) * n_recv]
            real += src_real * rec_real + src_imag * rec_imag
            imag += src_real * rec_imag - src_imag * rec_real
        cross = jnp.concatenate([real, imag], axis=0).astype(jnp.bfloat16)
        lagged = jnp.dot(lag_ref[...], cross, preferred_element_type=jnp.float32)
        lagged = lagged.astype(jnp.bfloat16).T
        send_buf[:, j] = lagged.reshape(n_chan, CH_DEV, LAGS)

    pl.semaphore_wait(barrier, jnp.where(keeps, n_chan - 1, n_chan))
    own = jnp.where(keeps, 2 * (me - first) + side, n_chan - 1)

    def send(slot):
        return pltpu.make_async_remote_copy(
            src_ref=send_buf.at[slot],
            dst_ref=recv_buf.at[me],
            send_sem=send_sems.at[slot],
            recv_sem=recv_sems.at[me],
            device_id=target(slot),
            device_id_type=pl.DeviceIdType.MESH,
        )

    def keep():
        return pltpu.make_async_copy(send_buf.at[own], recv_buf.at[me], recv_sems.at[me])

    sends = [send(lax.rem(own + hop, n_chan)) for hop in range(1, n_chan)]
    for copy in sends:
        copy.start()
    pl.when(keeps)(lambda: keep().start())
    pl.when(jnp.logical_not(keeps))(lambda: send(own).start())
    total = 0.0
    for k in range(n_chan):
        pltpu.make_async_copy(recv_buf.at[k], recv_buf.at[k], recv_sems.at[k]).wait()
        total += recv_buf[k].astype(jnp.float32)
    mean_square = jnp.sum(total * total, axis=-1, keepdims=True) * (1.0 / LAGS)
    out_ref[...] = total * lax.rsqrt(mean_square + 1e-06)
    for copy in sends:
        copy.wait_send()
    pl.when(jnp.logical_not(keeps))(lambda: send(own).wait_send())


def segment_shards(n_chan, n_grp, record, group_lengths, source_pick):
    rows, n_ch = record.shape
    dft = jnp.asarray(dft_rows(), jnp.bfloat16)
    lag = jnp.asarray(lag_rows().T, jnp.bfloat16)
    operands = (record, group_lengths, source_pick, dft, lag)
    block = (STEPS, CH_DEV, LAGS)
    return pl.pallas_call(
        functools.partial(partial_kernel, n_chan, n_grp),
        out_shape=jax.ShapeDtypeStruct(block, jnp.float32),
        in_specs=[pl.BlockSpec(memory_space=pltpu.HBM)] * 5,
        out_specs=pl.BlockSpec(memory_space=pltpu.VMEM),
        scratch_shapes=[
            pltpu.VMEM((STEPS, GROUPS), jnp.int32),
            pltpu.VMEM((STEPS, GROUPS), jnp.int32),
            pltpu.VMEM((rows, n_ch), jnp.bfloat16),
            pltpu.VMEM(dft.shape, jnp.bfloat16),
            pltpu.VMEM(lag.shape, jnp.bfloat16),
            pltpu.VMEM((n_chan,) + block, jnp.bfloat16),
            pltpu.VMEM((n_chan,) + block, jnp.bfloat16),
            pltpu.SemaphoreType.DMA((5,)),
            pltpu.SemaphoreType.DMA((n_chan,)),
            pltpu.SemaphoreType.DMA((n_chan,)),
        ],
        compiler_params=pltpu.CompilerParams(
            collective_id=0, has_side_effects=True, vmem_limit_bytes=32 * 1024 * 1024
        ),
    )(*(pltpu.with_memory_space_constraint(x, pltpu.HBM) for x in operands))


def solution(mesh):
    n_chan, n_grp = mesh.shape["chan"], mesh.shape["grp"]

    def local(record, group_lengths, source_pick):
        rows = record.shape[0]
        if rows % SAMP == 0 and n_chan * CH_DEV % 128 == 0 and n_grp % 2 == 0:
            return segment_shards(n_chan, n_grp, record, group_lengths, source_pick)
        return shards(record, group_lengths, source_pick)

    return jax.shard_map(
        local,
        mesh=mesh,
        in_specs=(P("chan", None), P(), P()),
        out_specs=P(None, ("chan", "grp"), None),
        check_vma=False,
    )
```

```python
import functools
import math

import jax
import jax.numpy as jnp
import numpy as np
from jax import lax
from jax.experimental import pallas as pl
from jax.experimental.pallas import tpu as pltpu
from jax.sharding import PartitionSpec as P

CH_DEV = 16
SEG = 32
SAMP = 200
LAGS = 128
STEPS = 4
GROUPS = 16
BINS = 101


def extended(array, sides, width):
    for axis, dim in sides:
        count, length = (lax.axis_size(axis), array.shape[dim])
        up = [(i, (i + 1) % count) for i in range(count - 1)]
        down = [(j, i) for i, j in up]
        last = lax.slice_in_dim(array, length - width, length, axis=dim)
        first = lax.slice_in_dim(array, 0, width, axis=dim)
        before = lax.ppermute(last, axis, up)
        after = lax.ppermute(first, axis, down)
        array = jnp.concatenate([before, array, after], axis=dim)
    return array


def dft_table(samples_count, bins_count):
    samples = jnp.arange(samples_count, dtype=jnp.int32)[:, None]
    freqs = jnp.arange(2 * bins_count, dtype=jnp.int32)[None, :]
    folded = jnp.where(freqs < bins_count, freqs, freqs - bins_count)
    phase = (samples * folded % samples_count).astype(jnp.float32) * (2.0 * math.pi / samples_count)
    return jnp.where(freqs < bins_count, jnp.cos(phase), -jnp.sin(phase)).astype(jnp.bfloat16)


def lag_table(samples_count, bins_count, lag_count):
    freq_rows = jnp.arange(2 * bins_count, dtype=jnp.int32)[:, None]
    lag_cols = jnp.arange(lag_count, dtype=jnp.int32)[None, :] - lag_count // 2
    folded = jnp.where(freq_rows < bins_count, freq_rows, freq_rows - bins_count)
    phase = (folded * lag_cols % samples_count).astype(jnp.float32) * (
        2.0 * math.pi / samples_count
    )
    weights = jnp.where((folded == 0) | (folded == samples_count // 2), 1.0, 2.0).astype(
        jnp.float32
    )
    return weights * jnp.where(freq_rows < bins_count, jnp.cos(phase), -jnp.sin(phase))


def whiten(strain):
    values = strain.astype(jnp.float32).reshape(SEG, SAMP, strain.shape[1])
    means = jnp.mean(values, axis=1, keepdims=True)
    centered = values - means
    mean_square = jnp.mean(centered * centered, axis=1, keepdims=True)
    return (centered / jnp.sqrt(mean_square + 1e-06)).astype(jnp.bfloat16)


def spectral(left, right):
    return jnp.einsum("ksf,sfc->fkc", left, right, preferred_element_type=jnp.float32)


def shards(record, group_lengths, source_pick):
    group_rank = lax.axis_index("grp")
    columns = lax.all_to_all(record, "chan", split_axis=1, concat_axis=0, tiled=True)
    mine = lax.dynamic_slice_in_dim(columns, group_rank * CH_DEV, CH_DEV, 1)
    padded = extended(mine, ((("chan", "grp"), 1),), 1)
    window = padded.astype(jnp.float32)
    strain = ((window[:, 2:] - window[:, :-2]) * 0.5).astype(jnp.bfloat16)
    whitened = whiten(strain)
    spectra = jnp.einsum(
        "snc,nk->skc", whitened, dft_table(SAMP, BINS), preferred_element_type=jnp.float32
    ).astype(jnp.bfloat16)
    first_channel = lax.axis_index(("chan", "grp")) * CH_DEV
    order = jnp.arange(GROUPS, dtype=jnp.int32)
    up_to = order[None, :] <= order[:, None]
    finish = jnp.sum(jnp.where(up_to[None], group_lengths[:, None, :], 0), axis=2)
    starts = finish - group_lengths
    source = starts + group_lengths * source_pick // 65536
    channels = first_channel + jnp.arange(CH_DEV, dtype=jnp.int32)
    owned = (source.reshape(1, -1) == channels[:, None]).astype(jnp.bfloat16)
    partial_table = jnp.einsum("skc,cj->skj", spectra, owned, preferred_element_type=jnp.float32)
    summed = lax.psum(partial_table, ("chan", "grp"))
    source_spec = jnp.transpose(summed.astype(jnp.bfloat16), (2, 0, 1))
    source_spec = source_spec.reshape(STEPS, GROUPS, SEG, 2 * BINS)
    lagt = lag_table(SAMP, BINS, LAGS)
    rec_real = spectra[:, :BINS]
    rec_imag = spectra[:, BINS:]
    traces = []
    for step_index in range(STEPS):
        source_now = source_spec[step_index]
        src_real = source_now[..., :BINS]
        src_imag = source_now[..., BINS:]
        real_all = spectral(src_real, rec_real) + spectral(src_imag, rec_imag)
        imag_all = spectral(src_real, rec_imag) - spectral(src_imag, rec_real)
        members = (
            (channels[None, :] >= starts[step_index][:, None])
            & (channels[None, :] < finish[step_index][:, None])
        ).astype(jnp.float32)
        cross_real = jnp.sum(real_all * members[None], axis=1)
        cross_imag = jnp.sum(imag_all * members[None], axis=1)
        cross_spectrum = jnp.concatenate([cross_real, cross_imag], axis=0)
        lagged = jnp.dot(
            cross_spectrum.T,
            lagt,
            precision=lax.Precision.HIGHEST,
            preferred_element_type=jnp.float32,
        )
        inverse_rms = 1.0 / jnp.sqrt(jnp.mean(lagged * lagged, axis=1, keepdims=True) + 1e-06)
        traces.append(lagged * inverse_rms)
    return jnp.stack(traces)


HALF = 128
SRC = STEPS * GROUPS
WINDOW = 208
EDGE = WINDOW - SAMP


def turns(rows, columns):
    phase = rows[:, None] * columns[None, :] % SAMP * (2.0 * math.pi / SAMP)
    pad = ((0, 0), (0, HALF - BINS)) if columns.size == BINS else ((0, HALF - BINS), (0, 0))
    return np.pad(np.cos(phase), pad), np.pad(-np.sin(phase), pad)


def dft_tables():
    table = np.concatenate(turns(np.arange(SAMP), np.arange(BINS)), axis=1)
    return np.stack([np.pad(table, ((k * EDGE, (1 - k) * EDGE), (0, 0))) for k in range(2)])


def lag_rows():
    freqs = np.arange(BINS)
    weights = np.where((freqs == 0) | (freqs == SAMP // 2), 1.0, 2.0)
    weights = np.pad(weights, (0, HALF - BINS))[:, None]
    tables = turns(freqs, np.arange(LAGS) - LAGS // 2)
    return np.concatenate([weights * table for table in tables], axis=0)


def window_of(seg):
    return seg * SAMP - seg % 2 * EDGE


def partial_kernel(
    n_chan,
    n_grp,
    rec_hbm,
    lengths_hbm,
    pick_hbm,
    dft_hbm,
    lag_hbm,
    out_ref,
    lengths_ref,
    pick_ref,
    rec_buf,
    dft_ref,
    lag_ref,
    send_buf,
    recv_buf,
    load_sems,
    send_sem,
    recv_sem,
):
    rows, n_ch = rec_buf.shape
    segs = rows // SAMP
    n_recv = n_chan * CH_DEV
    half = n_chan // 2
    me, group = lax.axis_index("chan"), lax.axis_index("grp")
    pair, side = group // 2, group % 2
    first = (1 - side) * half
    want = jnp.where(me < half, 1, 0)
    keeps = side == want
    source_grp = pair * 2 + want

    def target(slot):
        return (first + slot // 2, pair * 2 + slot % 2)

    cuts = [0, rows]
    parts = [(rec_hbm.at[pl.ds(a, b - a)], rec_buf.at[pl.ds(a, b - a)]) for a, b in zip(cuts, cuts[1:])]
    loads = [
        pltpu.make_async_copy(src, dst, load_sems.at[i])
        for i, (src, dst) in enumerate(
            [(lengths_hbm, lengths_ref), (pick_hbm, pick_ref)]
            + parts[:1]
            + [(dft_hbm, dft_ref)]
            + parts[1:]
            + [(lag_hbm, lag_ref)]
        )
    ]
    for load in loads:
        load.start()
    small, dft_load, lag_load = loads[:2], loads[3], loads[-1]
    parts = loads[2:3] + loads[4:-1]
    barrier = pltpu.get_barrier_semaphore()

    def greet(chan):
        pl.semaphore_signal(
            barrier,
            inc=1,
            device_id=(chan, source_grp),
            device_id_type=pl.DeviceIdType.MESH,
        )

    for hop in range(1, n_chan):
        greet(lax.rem(me + hop, n_chan))
    pl.when(jnp.logical_not(keeps))(lambda: greet(me))

    place = lax.broadcasted_iota(jnp.int32, (n_recv, 1), 0)
    slot_chan, slot_grp = target(place // CH_DEV)
    receivers = (slot_chan * n_grp + slot_grp) * CH_DEV + place % CH_DEV

    def gauge_of(channels):
        apart = lax.broadcasted_iota(jnp.int32, (channels.shape[0], n_ch), 1) - channels
        return jnp.where(apart == 1, 0.5, jnp.where(apart == -1, -0.5, 0.0)).astype(jnp.bfloat16)

    recv_gauge = gauge_of(receivers)

    for copy in small:
        copy.wait()
    line = lax.broadcasted_iota(jnp.int32, (STEPS, 128), 1)
    group_of = line % GROUPS
    lengths, picks = lengths_ref[...], pick_ref[...]
    ends = jnp.zeros((STEPS, 128), jnp.int32)
    starts, finish, spots = ends, ends, ends
    for g in range(GROUPS):
        length = jnp.broadcast_to(lengths[:, g : g + 1], ends.shape)
        pick = jnp.broadcast_to(picks[:, g : g + 1], ends.shape)
        spots = jnp.where(group_of == g, ends + lax.shift_right_logical(length * pick, 16), spots)
        starts = jnp.where(group_of == g, ends, starts)
        ends = ends + length
        finish = jnp.where(group_of == g, ends, finish)
    own_step = lax.broadcasted_iota(jnp.int32, ends.shape, 0) == line // GROUPS

    def in_line(table):
        return jnp.sum(jnp.where(own_step, table, 0), axis=0, keepdims=True)

    starts, finish = in_line(starts)[:, :SRC], in_line(finish)[:, :SRC]
    down = lax.broadcasted_iota(jnp.int32, (SRC, 128), 0)
    along = lax.broadcasted_iota(jnp.int32, (SRC, 128), 1)
    sources = jnp.where(down == along, in_line(spots).astype(jnp.float32), 0.0)
    sources = jnp.sum(sources, axis=1, keepdims=True).astype(jnp.int32)
    gauge = jnp.concatenate([recv_gauge, gauge_of(sources)], axis=0)
    member = (starts <= receivers) & (receivers < finish)
    step_of = lax.broadcasted_iota(jnp.int32, (n_recv, SRC), 1) // GROUPS
    spread = jnp.concatenate(
        [jnp.where(member & (step_of == j), 1.0, 0.0) for j in range(STEPS)], axis=0
    ).astype(jnp.bfloat16)

    lanes = lax.broadcasted_iota(jnp.int32, (n_recv + SRC, WINDOW), 1)

    def strain_of(seg):
        window = rec_buf[pl.ds(window_of(seg), WINDOW)]
        return lax.dot_general(
            gauge, window, (((1,), (1,)), ((), ())), preferred_element_type=jnp.float32
        )

    def spectra_of(seg, strain):
        head = seg % 2 * EDGE
        within = (lanes >= head) & (lanes < head + SAMP)
        values = strain.astype(jnp.bfloat16)
        wide = values.astype(jnp.float32)
        mean = jnp.sum(jnp.where(within, wide, 0.0), axis=1, keepdims=True) * (1.0 / SAMP)
        centered = jnp.where(within, wide - mean, 0.0)
        mean_square = jnp.sum(centered * centered, axis=1, keepdims=True) * (1.0 / SAMP)
        whitened = (centered * lax.rsqrt(mean_square + 1e-06)).astype(jnp.bfloat16)
        spec = jnp.dot(whitened, dft_ref[seg % 2], preferred_element_type=jnp.float32)
        spec = spec.astype(jnp.bfloat16)
        return spec[:, :HALF], spec[:, HALF:]

    crosses = [[None, None] for _ in range(STEPS)]

    def add_cross(spec):
        real, imag = spec
        src = jnp.concatenate([real[n_recv:], imag[n_recv:]], axis=1)
        src = jnp.dot(spread, src, preferred_element_type=jnp.float32)
        rec_real, rec_imag = real[:n_recv].astype(jnp.float32), imag[:n_recv].astype(jnp.float32)
        for j in range(STEPS):
            src_real = src[j * n_recv : (j + 1) * n_recv, :HALF]
            src_imag = src[j * n_recv : (j + 1) * n_recv, HALF:]
            terms = (
                src_real * rec_real + src_imag * rec_imag,
                src_real * rec_imag - src_imag * rec_real,
            )
            for part, term in enumerate(terms):
                so_far = crosses[j][part]
                crosses[j][part] = term if so_far is None else so_far + term

    for part in parts + [dft_load, lag_load]:
        part.wait()
    strains = [strain_of(seg) for seg in range(segs)]
    specs = [spectra_of(seg, strains[seg]) for seg in range(segs)]
    for spec in specs:
        add_cross(spec)
    for j in range(STEPS):
        cross = jnp.concatenate(crosses[j], axis=1).astype(jnp.bfloat16)
        lagged = jnp.dot(cross, lag_ref[...], preferred_element_type=jnp.float32)
        send_buf[:, j] = lagged.astype(jnp.bfloat16).reshape(n_chan, CH_DEV, LAGS)

    pl.semaphore_wait(barrier, jnp.where(keeps, n_chan - 1, n_chan))
    own = jnp.where(keeps, 2 * (me - first) + side, n_chan - 1)

    def send(slot):
        return pltpu.make_async_remote_copy(
            src_ref=send_buf.at[slot],
            dst_ref=recv_buf.at[me],
            send_sem=send_sem,
            recv_sem=recv_sem,
            device_id=target(slot),
            device_id_type=pl.DeviceIdType.MESH,
        )

    for hop in range(1, n_chan):
        send(lax.rem(own + hop, n_chan)).start()
    pl.when(keeps)(
        lambda: pltpu.make_async_copy(send_buf.at[own], recv_buf.at[me], recv_sem).start()
    )
    pl.when(jnp.logical_not(keeps))(lambda: send(own).start())
    pltpu.make_async_copy(recv_buf, recv_buf, recv_sem).wait()
    total = jnp.sum(recv_buf[...].astype(jnp.float32), axis=0)
    mean_square = jnp.sum(total * total, axis=-1, keepdims=True) * (1.0 / LAGS)
    out_ref[...] = total * lax.rsqrt(mean_square + 1e-06)
    most = send_buf.at[pl.ds(0, n_chan - 1)]
    pltpu.make_async_copy(most, most, send_sem).wait()
    pl.when(jnp.logical_not(keeps))(
        lambda: pltpu.make_async_copy(send_buf.at[0], send_buf.at[0], send_sem).wait()
    )


def segment_shards(n_chan, n_grp, record, group_lengths, source_pick):
    rows, n_ch = record.shape
    dft = jnp.asarray(dft_tables(), jnp.bfloat16)
    lag = jnp.asarray(lag_rows(), jnp.bfloat16)
    operands = (record, group_lengths, source_pick, dft, lag)
    block = (STEPS, CH_DEV, LAGS)
    return pl.pallas_call(
        functools.partial(partial_kernel, n_chan, n_grp),
        out_shape=jax.ShapeDtypeStruct(block, jnp.float32),
        in_specs=[pl.BlockSpec(memory_space=pltpu.HBM)] * 5,
        out_specs=pl.BlockSpec(memory_space=pltpu.VMEM),
        scratch_shapes=[
            pltpu.VMEM((STEPS, GROUPS), jnp.int32),
            pltpu.VMEM((STEPS, GROUPS), jnp.int32),
            pltpu.VMEM((rows, n_ch), jnp.bfloat16),
            pltpu.VMEM(dft.shape, jnp.bfloat16),
            pltpu.VMEM(lag.shape, jnp.bfloat16),
            pltpu.VMEM((n_chan,) + block, jnp.bfloat16),
            pltpu.VMEM((n_chan,) + block, jnp.bfloat16),
            pltpu.SemaphoreType.DMA((4 + rows // SAMP,)),
            pltpu.SemaphoreType.DMA,
            pltpu.SemaphoreType.DMA,
        ],
        compiler_params=pltpu.CompilerParams(
            collective_id=0, has_side_effects=True, vmem_limit_bytes=32 * 1024 * 1024
        ),
    )(*(pltpu.with_memory_space_constraint(x, pltpu.HBM) for x in operands))


def solution(mesh):
    n_chan, n_grp = mesh.shape["chan"], mesh.shape["grp"]

    def local(record, group_lengths, source_pick):
        rows = record.shape[0]
        if rows % (2 * SAMP) == 0 and n_chan * CH_DEV % 128 == 0 and n_grp % 2 == 0:
            return segment_shards(n_chan, n_grp, record, group_lengths, source_pick)
        return shards(record, group_lengths, source_pick)

    return jax.shard_map(
        local,
        mesh=mesh,
        in_specs=(P("chan", None), P(), P()),
        out_specs=P(None, ("chan", "grp"), None),
        check_vma=False,
    )
```

```python
import functools
import math

import jax
import jax.numpy as jnp
import numpy as np
from jax import lax
from jax.experimental import pallas as pl
from jax.experimental.pallas import tpu as pltpu
from jax.sharding import PartitionSpec as P

CH_DEV = 16
SEG = 32
SAMP = 200
LAGS = 128
STEPS = 4
GROUPS = 16
BINS = 101


def extended(array, sides, width):
    for axis, dim in sides:
        count, length = (lax.axis_size(axis), array.shape[dim])
        up = [(i, (i + 1) % count) for i in range(count - 1)]
        down = [(j, i) for i, j in up]
        last = lax.slice_in_dim(array, length - width, length, axis=dim)
        first = lax.slice_in_dim(array, 0, width, axis=dim)
        before = lax.ppermute(last, axis, up)
        after = lax.ppermute(first, axis, down)
        array = jnp.concatenate([before, array, after], axis=dim)
    return array


def dft_table(samples_count, bins_count):
    samples = jnp.arange(samples_count, dtype=jnp.int32)[:, None]
    freqs = jnp.arange(2 * bins_count, dtype=jnp.int32)[None, :]
    folded = jnp.where(freqs < bins_count, freqs, freqs - bins_count)
    phase = (samples * folded % samples_count).astype(jnp.float32) * (2.0 * math.pi / samples_count)
    return jnp.where(freqs < bins_count, jnp.cos(phase), -jnp.sin(phase)).astype(jnp.bfloat16)


def lag_table(samples_count, bins_count, lag_count):
    freq_rows = jnp.arange(2 * bins_count, dtype=jnp.int32)[:, None]
    lag_cols = jnp.arange(lag_count, dtype=jnp.int32)[None, :] - lag_count // 2
    folded = jnp.where(freq_rows < bins_count, freq_rows, freq_rows - bins_count)
    phase = (folded * lag_cols % samples_count).astype(jnp.float32) * (
        2.0 * math.pi / samples_count
    )
    weights = jnp.where((folded == 0) | (folded == samples_count // 2), 1.0, 2.0).astype(
        jnp.float32
    )
    return weights * jnp.where(freq_rows < bins_count, jnp.cos(phase), -jnp.sin(phase))


def whiten(strain):
    values = strain.astype(jnp.float32).reshape(SEG, SAMP, strain.shape[1])
    means = jnp.mean(values, axis=1, keepdims=True)
    centered = values - means
    mean_square = jnp.mean(centered * centered, axis=1, keepdims=True)
    return (centered / jnp.sqrt(mean_square + 1e-06)).astype(jnp.bfloat16)


def spectral(left, right):
    return jnp.einsum("ksf,sfc->fkc", left, right, preferred_element_type=jnp.float32)


def shards(record, group_lengths, source_pick):
    group_rank = lax.axis_index("grp")
    columns = lax.all_to_all(record, "chan", split_axis=1, concat_axis=0, tiled=True)
    mine = lax.dynamic_slice_in_dim(columns, group_rank * CH_DEV, CH_DEV, 1)
    padded = extended(mine, ((("chan", "grp"), 1),), 1)
    window = padded.astype(jnp.float32)
    strain = ((window[:, 2:] - window[:, :-2]) * 0.5).astype(jnp.bfloat16)
    whitened = whiten(strain)
    spectra = jnp.einsum(
        "snc,nk->skc", whitened, dft_table(SAMP, BINS), preferred_element_type=jnp.float32
    ).astype(jnp.bfloat16)
    first_channel = lax.axis_index(("chan", "grp")) * CH_DEV
    order = jnp.arange(GROUPS, dtype=jnp.int32)
    up_to = order[None, :] <= order[:, None]
    finish = jnp.sum(jnp.where(up_to[None], group_lengths[:, None, :], 0), axis=2)
    starts = finish - group_lengths
    source = starts + group_lengths * source_pick // 65536
    channels = first_channel + jnp.arange(CH_DEV, dtype=jnp.int32)
    owned = (source.reshape(1, -1) == channels[:, None]).astype(jnp.bfloat16)
    partial_table = jnp.einsum("skc,cj->skj", spectra, owned, preferred_element_type=jnp.float32)
    summed = lax.psum(partial_table, ("chan", "grp"))
    source_spec = jnp.transpose(summed.astype(jnp.bfloat16), (2, 0, 1))
    source_spec = source_spec.reshape(STEPS, GROUPS, SEG, 2 * BINS)
    lagt = lag_table(SAMP, BINS, LAGS)
    rec_real = spectra[:, :BINS]
    rec_imag = spectra[:, BINS:]
    traces = []
    for step_index in range(STEPS):
        source_now = source_spec[step_index]
        src_real = source_now[..., :BINS]
        src_imag = source_now[..., BINS:]
        real_all = spectral(src_real, rec_real) + spectral(src_imag, rec_imag)
        imag_all = spectral(src_real, rec_imag) - spectral(src_imag, rec_real)
        members = (
            (channels[None, :] >= starts[step_index][:, None])
            & (channels[None, :] < finish[step_index][:, None])
        ).astype(jnp.float32)
        cross_real = jnp.sum(real_all * members[None], axis=1)
        cross_imag = jnp.sum(imag_all * members[None], axis=1)
        cross_spectrum = jnp.concatenate([cross_real, cross_imag], axis=0)
        lagged = jnp.dot(
            cross_spectrum.T,
            lagt,
            precision=lax.Precision.HIGHEST,
            preferred_element_type=jnp.float32,
        )
        inverse_rms = 1.0 / jnp.sqrt(jnp.mean(lagged * lagged, axis=1, keepdims=True) + 1e-06)
        traces.append(lagged * inverse_rms)
    return jnp.stack(traces)


HALF = 128
LANES = 128
SRC = STEPS * GROUPS
WINDOW = 208
EDGE = WINDOW - SAMP
FAR = 2
EARLY = 2


def turns(rows, columns):
    phase = rows[:, None] * columns[None, :] % SAMP * (2.0 * math.pi / SAMP)
    pad = ((0, 0), (0, HALF - BINS)) if columns.size == BINS else ((0, HALF - BINS), (0, 0))
    return np.pad(np.cos(phase), pad), np.pad(-np.sin(phase), pad)


def dft_rows():
    return np.concatenate(turns(np.arange(WINDOW), np.arange(BINS)), axis=1)


def lag_rows():
    freqs = np.arange(BINS)
    weights = np.where((freqs == 0) | (freqs == SAMP // 2), 1.0, 2.0)
    weights = np.pad(weights, (0, HALF - BINS))[:, None]
    tables = turns(freqs, np.arange(LAGS) - LAGS // 2)
    return np.concatenate([weights * table for table in tables], axis=0)


def window_of(seg):
    return seg * SAMP - seg % 2 * EDGE


def partial_kernel(
    n_chan,
    n_grp,
    rec_hbm,
    lengths_hbm,
    pick_hbm,
    dft_hbm,
    lag_hbm,
    out_ref,
    lengths_ref,
    pick_ref,
    rec_buf,
    dft_ref,
    lag_ref,
    send_buf,
    recv_buf,
    load_sems,
    send_sem,
    recv_sem,
):
    rows, n_ch = rec_buf.shape
    segs = rows // SAMP
    n_recv = n_chan * CH_DEV
    half = n_chan // 2
    me, group = lax.axis_index("chan"), lax.axis_index("grp")
    pair, side = group // 2, group % 2
    first = (1 - side) * half
    want = jnp.where(me < half, 1, 0)
    keeps = side == want
    source_grp = pair * 2 + want

    def target(slot):
        return (first + slot // 2, pair * 2 + slot % 2)

    loads = [
        pltpu.make_async_copy(src, dst, load_sems.at[i])
        for i, (src, dst) in enumerate(
            [
                (lengths_hbm, lengths_ref),
                (pick_hbm, pick_ref),
                (rec_hbm, rec_buf),
                (dft_hbm, dft_ref),
                (lag_hbm, lag_ref),
            ]
        )
    ]
    for load in loads:
        load.start()
    small, large = loads[:2], loads[2:]
    barrier = pltpu.get_barrier_semaphore()

    def greet(chan):
        pl.semaphore_signal(
            barrier,
            inc=1,
            device_id=(chan, source_grp),
            device_id_type=pl.DeviceIdType.MESH,
        )

    for hop in range(1, n_chan):
        greet(lax.rem(me + hop, n_chan))
    pl.when(jnp.logical_not(keeps))(lambda: greet(me))

    place = lax.broadcasted_iota(jnp.int32, (n_recv, 1), 0)
    slot_chan, slot_grp = target(place // CH_DEV)
    receivers = (slot_chan * n_grp + slot_grp) * CH_DEV + place % CH_DEV

    def gauge_of(channels):
        apart = lax.broadcasted_iota(jnp.int32, (channels.shape[0], n_ch), 1) - channels
        return jnp.where(apart == 1, 0.5, jnp.where(apart == -1, -0.5, 0.0)).astype(jnp.bfloat16)

    recv_gauge = gauge_of(receivers)

    for copy in small:
        copy.wait()
    line = lax.broadcasted_iota(jnp.int32, (STEPS, 128), 1)
    group_of = line % GROUPS
    lengths, picks = lengths_ref[...], pick_ref[...]
    ends = jnp.zeros((STEPS, 128), jnp.int32)
    starts, finish, spots = ends, ends, ends
    for g in range(GROUPS):
        length = jnp.broadcast_to(lengths[:, g : g + 1], ends.shape)
        pick = jnp.broadcast_to(picks[:, g : g + 1], ends.shape)
        spots = jnp.where(group_of == g, ends + lax.shift_right_logical(length * pick, 16), spots)
        starts = jnp.where(group_of == g, ends, starts)
        ends = ends + length
        finish = jnp.where(group_of == g, ends, finish)
    own_step = lax.broadcasted_iota(jnp.int32, ends.shape, 0) == line // GROUPS

    def in_line(table):
        return jnp.sum(jnp.where(own_step, table, 0), axis=0, keepdims=True)

    starts, finish = in_line(starts)[:, :SRC], in_line(finish)[:, :SRC]
    down = lax.broadcasted_iota(jnp.int32, (SRC, 128), 0)
    along = lax.broadcasted_iota(jnp.int32, (SRC, 128), 1)
    sources = jnp.where(down == along, in_line(spots).astype(jnp.float32), 0.0)
    sources = jnp.sum(sources, axis=1, keepdims=True).astype(jnp.int32)
    member = (starts <= receivers) & (receivers < finish)
    step_of = lax.broadcasted_iota(jnp.int32, (n_recv, SRC), 1) // GROUPS
    lanes = lax.broadcasted_iota(jnp.int32, (1, WINDOW), 1)

    def strain_of(gauge, seg):
        window = rec_buf[pl.ds(window_of(seg), WINDOW)]
        return lax.dot_general(
            gauge, window, (((1,), (1,)), ((), ())), preferred_element_type=jnp.float32
        )

    def within(seg, series):
        if seg % 2 == 0:
            tail = jnp.where(lanes[:, LANES:] < SAMP, series[:, LANES:], 0.0)
            return jnp.concatenate([series[:, :LANES], tail], axis=1)
        head = jnp.where(lanes[:, :LANES] >= EDGE, series[:, :LANES], 0.0)
        return jnp.concatenate([head, series[:, LANES:]], axis=1)

    def center_of(seg, strain):
        wide = strain.astype(jnp.bfloat16).astype(jnp.float32)
        mean = jnp.sum(within(seg, wide), axis=1, keepdims=True) * (1.0 / SAMP)
        centered = within(seg, wide - mean)
        mean_square = jnp.sum(centered * centered, axis=1, keepdims=True) * (1.0 / SAMP)
        return centered.astype(jnp.bfloat16), lax.rsqrt(mean_square + 1e-06)

    def spectra_of(strains):
        parts = [center_of(seg, strain) for seg, strain in enumerate(strains)]
        series = jnp.concatenate([part[0] for part in parts], axis=0)
        spec = jnp.dot(series, dft_ref[...], preferred_element_type=jnp.float32)
        specs, count = [], strains[0].shape[0]
        for seg, (_, scale) in enumerate(parts):
            part = spec[seg * count : (seg + 1) * count]
            specs.append((part * scale).astype(jnp.bfloat16))
        return specs

    def correlate(slots, receivers, sources):
        begin, end = slots.start * CH_DEV, slots.stop * CH_DEV
        count = end - begin
        spread = jnp.concatenate(
            [jnp.where(member[begin:end] & (step_of[begin:end] == j), 1.0, 0.0) for j in range(STEPS)],
            axis=0,
        ).astype(jnp.bfloat16)
        crosses = [[0.0, 0.0] for _ in range(STEPS)]
        for receiver, source in zip(receivers, sources):
            source = jnp.dot(spread, source, preferred_element_type=jnp.float32)
            rec_real = receiver[:, :HALF].astype(jnp.float32)
            rec_imag = receiver[:, HALF:].astype(jnp.float32)
            for j in range(STEPS):
                src_real = source[j * count : (j + 1) * count, :HALF]
                src_imag = source[j * count : (j + 1) * count, HALF:]
                crosses[j][0] += src_real * rec_real + src_imag * rec_imag
                crosses[j][1] += src_real * rec_imag - src_imag * rec_real
        cross = [jnp.concatenate(parts, axis=1).astype(jnp.bfloat16) for parts in crosses]
        lagged = jnp.dot(
            jnp.concatenate(cross, axis=0), lag_ref[...], preferred_element_type=jnp.float32
        ).astype(jnp.bfloat16)
        for j in range(STEPS):
            block = lagged[j * count : (j + 1) * count].reshape(len(slots), CH_DEV, LAGS)
            send_buf[pl.ds(slots.start, len(slots)), j] = block

    own = jnp.where(keeps, 2 * (me - first) + side, n_chan)
    far = jnp.where(me < n_chan - FAR, 0, 1)

    def send(slot):
        return pltpu.make_async_remote_copy(
            src_ref=send_buf.at[slot],
            dst_ref=recv_buf.at[me],
            send_sem=send_sem,
            recv_sem=recv_sem.at[far],
            device_id=target(slot),
            device_id_type=pl.DeviceIdType.MESH,
        )

    def hand_out(slots):
        for slot in slots:
            pl.when(own != slot)(lambda: send(slot).start())
        pl.when((own >= slots.start) & (own < slots.stop))(
            lambda: pltpu.make_async_copy(send_buf.at[own], recv_buf.at[me], recv_sem.at[far]).start()
        )

    early, late = range(EARLY), range(EARLY, n_chan)
    split = EARLY * CH_DEV
    for load in large:
        load.wait()
    front = jnp.concatenate([recv_gauge[:split], gauge_of(sources)], axis=0)
    strains = [strain_of(front, seg) for seg in range(segs)]
    specs = spectra_of(strains)
    spec_sources = [spec[split:] for spec in specs]
    correlate(early, [spec[:split] for spec in specs], spec_sources)

    def enter():
        pl.semaphore_wait(barrier, jnp.where(keeps, n_chan - 1, n_chan))
        hand_out(early)

    pl.when(side == 1)(enter)
    strains = [strain_of(recv_gauge[split:], seg) for seg in range(segs)]
    specs = spectra_of(strains)
    correlate(late, specs, spec_sources)
    pl.when(side == 0)(enter)
    hand_out(late)

    total = 0.0
    for k, chans in enumerate((pl.ds(0, n_chan - FAR), pl.ds(n_chan - FAR, FAR))):
        blocks = recv_buf.at[chans]
        pltpu.make_async_copy(blocks, blocks, recv_sem.at[k]).wait()
        total += jnp.sum(blocks[...].astype(jnp.float32), axis=0)
    mean_square = jnp.sum(total * total, axis=-1, keepdims=True) * (1.0 / LAGS)
    out_ref[...] = total * lax.rsqrt(mean_square + 1e-06)
    most = send_buf.at[pl.ds(0, n_chan - 1)]
    pltpu.make_async_copy(most, most, send_sem).wait()
    pl.when(jnp.logical_not(keeps))(
        lambda: pltpu.make_async_copy(send_buf.at[0], send_buf.at[0], send_sem).wait()
    )


def segment_shards(n_chan, n_grp, record, group_lengths, source_pick):
    rows, n_ch = record.shape
    dft = jnp.asarray(dft_rows(), jnp.bfloat16)
    lag = jnp.asarray(lag_rows(), jnp.bfloat16)
    operands = (record, group_lengths, source_pick, dft, lag)
    block = (STEPS, CH_DEV, LAGS)
    return pl.pallas_call(
        functools.partial(partial_kernel, n_chan, n_grp),
        out_shape=jax.ShapeDtypeStruct(block, jnp.float32),
        in_specs=[pl.BlockSpec(memory_space=pltpu.HBM)] * 5,
        out_specs=pl.BlockSpec(memory_space=pltpu.VMEM),
        scratch_shapes=[
            pltpu.VMEM((STEPS, GROUPS), jnp.int32),
            pltpu.VMEM((STEPS, GROUPS), jnp.int32),
            pltpu.VMEM((rows, n_ch), jnp.bfloat16),
            pltpu.VMEM(dft.shape, jnp.bfloat16),
            pltpu.VMEM(lag.shape, jnp.bfloat16),
            pltpu.VMEM((n_chan,) + block, jnp.bfloat16),
            pltpu.VMEM((n_chan,) + block, jnp.bfloat16),
            pltpu.SemaphoreType.DMA((5,)),
            pltpu.SemaphoreType.DMA,
            pltpu.SemaphoreType.DMA((2,)),
        ],
        compiler_params=pltpu.CompilerParams(
            collective_id=0, has_side_effects=True, vmem_limit_bytes=32 * 1024 * 1024
        ),
    )(*(pltpu.with_memory_space_constraint(x, pltpu.HBM) for x in operands))


def solution(mesh):
    n_chan, n_grp = mesh.shape["chan"], mesh.shape["grp"]

    def local(record, group_lengths, source_pick):
        rows = record.shape[0]
        if rows % (2 * SAMP) == 0 and n_chan * CH_DEV % 128 == 0 and n_grp % 2 == 0:
            return segment_shards(n_chan, n_grp, record, group_lengths, source_pick)
        return shards(record, group_lengths, source_pick)

    return jax.shard_map(
        local,
        mesh=mesh,
        in_specs=(P("chan", None), P(), P()),
        out_specs=P(None, ("chan", "grp"), None),
        check_vma=False,
    )
```

```python
import functools
import math

import jax
import jax.numpy as jnp
import numpy as np
from jax import lax
from jax.experimental import pallas as pl
from jax.experimental.pallas import tpu as pltpu
from jax.sharding import PartitionSpec as P

CH_DEV = 16
SEG = 32
SAMP = 200
LAGS = 128
STEPS = 4
GROUPS = 16
BINS = 101


def extended(array, sides, width):
    for axis, dim in sides:
        count, length = (lax.axis_size(axis), array.shape[dim])
        up = [(i, (i + 1) % count) for i in range(count - 1)]
        down = [(j, i) for i, j in up]
        last = lax.slice_in_dim(array, length - width, length, axis=dim)
        first = lax.slice_in_dim(array, 0, width, axis=dim)
        before = lax.ppermute(last, axis, up)
        after = lax.ppermute(first, axis, down)
        array = jnp.concatenate([before, array, after], axis=dim)
    return array


def dft_table(samples_count, bins_count):
    samples = jnp.arange(samples_count, dtype=jnp.int32)[:, None]
    freqs = jnp.arange(2 * bins_count, dtype=jnp.int32)[None, :]
    folded = jnp.where(freqs < bins_count, freqs, freqs - bins_count)
    phase = (samples * folded % samples_count).astype(jnp.float32) * (2.0 * math.pi / samples_count)
    return jnp.where(freqs < bins_count, jnp.cos(phase), -jnp.sin(phase)).astype(jnp.bfloat16)


def lag_table(samples_count, bins_count, lag_count):
    freq_rows = jnp.arange(2 * bins_count, dtype=jnp.int32)[:, None]
    lag_cols = jnp.arange(lag_count, dtype=jnp.int32)[None, :] - lag_count // 2
    folded = jnp.where(freq_rows < bins_count, freq_rows, freq_rows - bins_count)
    phase = (folded * lag_cols % samples_count).astype(jnp.float32) * (
        2.0 * math.pi / samples_count
    )
    weights = jnp.where((folded == 0) | (folded == samples_count // 2), 1.0, 2.0).astype(
        jnp.float32
    )
    return weights * jnp.where(freq_rows < bins_count, jnp.cos(phase), -jnp.sin(phase))


def whiten(strain):
    values = strain.astype(jnp.float32).reshape(SEG, SAMP, strain.shape[1])
    means = jnp.mean(values, axis=1, keepdims=True)
    centered = values - means
    mean_square = jnp.mean(centered * centered, axis=1, keepdims=True)
    return (centered / jnp.sqrt(mean_square + 1e-06)).astype(jnp.bfloat16)


def spectral(left, right):
    return jnp.einsum("ksf,sfc->fkc", left, right, preferred_element_type=jnp.float32)


def shards(record, group_lengths, source_pick):
    group_rank = lax.axis_index("grp")
    columns = lax.all_to_all(record, "chan", split_axis=1, concat_axis=0, tiled=True)
    mine = lax.dynamic_slice_in_dim(columns, group_rank * CH_DEV, CH_DEV, 1)
    padded = extended(mine, ((("chan", "grp"), 1),), 1)
    window = padded.astype(jnp.float32)
    strain = ((window[:, 2:] - window[:, :-2]) * 0.5).astype(jnp.bfloat16)
    whitened = whiten(strain)
    spectra = jnp.einsum(
        "snc,nk->skc", whitened, dft_table(SAMP, BINS), preferred_element_type=jnp.float32
    ).astype(jnp.bfloat16)
    first_channel = lax.axis_index(("chan", "grp")) * CH_DEV
    order = jnp.arange(GROUPS, dtype=jnp.int32)
    up_to = order[None, :] <= order[:, None]
    finish = jnp.sum(jnp.where(up_to[None], group_lengths[:, None, :], 0), axis=2)
    starts = finish - group_lengths
    source = starts + group_lengths * source_pick // 65536
    channels = first_channel + jnp.arange(CH_DEV, dtype=jnp.int32)
    owned = (source.reshape(1, -1) == channels[:, None]).astype(jnp.bfloat16)
    partial_table = jnp.einsum("skc,cj->skj", spectra, owned, preferred_element_type=jnp.float32)
    summed = lax.psum(partial_table, ("chan", "grp"))
    source_spec = jnp.transpose(summed.astype(jnp.bfloat16), (2, 0, 1))
    source_spec = source_spec.reshape(STEPS, GROUPS, SEG, 2 * BINS)
    lagt = lag_table(SAMP, BINS, LAGS)
    rec_real = spectra[:, :BINS]
    rec_imag = spectra[:, BINS:]
    traces = []
    for step_index in range(STEPS):
        source_now = source_spec[step_index]
        src_real = source_now[..., :BINS]
        src_imag = source_now[..., BINS:]
        real_all = spectral(src_real, rec_real) + spectral(src_imag, rec_imag)
        imag_all = spectral(src_real, rec_imag) - spectral(src_imag, rec_real)
        members = (
            (channels[None, :] >= starts[step_index][:, None])
            & (channels[None, :] < finish[step_index][:, None])
        ).astype(jnp.float32)
        cross_real = jnp.sum(real_all * members[None], axis=1)
        cross_imag = jnp.sum(imag_all * members[None], axis=1)
        cross_spectrum = jnp.concatenate([cross_real, cross_imag], axis=0)
        lagged = jnp.dot(
            cross_spectrum.T,
            lagt,
            precision=lax.Precision.HIGHEST,
            preferred_element_type=jnp.float32,
        )
        inverse_rms = 1.0 / jnp.sqrt(jnp.mean(lagged * lagged, axis=1, keepdims=True) + 1e-06)
        traces.append(lagged * inverse_rms)
    return jnp.stack(traces)


HALF = 128
LANES = 128
SRC = STEPS * GROUPS
WINDOW = 208
EDGE = WINDOW - SAMP
FAR = 2
EARLY = 2


def turns(rows, columns):
    phase = rows[:, None] * columns[None, :] % SAMP * (2.0 * math.pi / SAMP)
    pad = ((0, 0), (0, HALF - BINS)) if columns.size == BINS else ((0, HALF - BINS), (0, 0))
    return np.pad(np.cos(phase), pad), np.pad(-np.sin(phase), pad)


def dft_rows():
    return np.concatenate(turns(np.arange(WINDOW), np.arange(BINS)), axis=1)


def lag_rows():
    freqs = np.arange(BINS)
    weights = np.where((freqs == 0) | (freqs == SAMP // 2), 1.0, 2.0)
    weights = np.pad(weights, (0, HALF - BINS))[:, None]
    tables = turns(freqs, np.arange(LAGS) - LAGS // 2)
    return np.concatenate([weights * table for table in tables], axis=0)


def near_columns(n_grp, n_ch):
    return -(-(n_grp * CH_DEV + n_ch // 16 + 1) // LANES) * LANES


def window_of(seg):
    return seg * SAMP - seg % 2 * EDGE


def partial_kernel(
    n_chan,
    n_grp,
    rec_hbm,
    lengths_hbm,
    pick_hbm,
    dft_hbm,
    lag_hbm,
    out_ref,
    lengths_ref,
    pick_ref,
    rec_buf,
    dft_ref,
    lag_ref,
    send_buf,
    recv_buf,
    load_sems,
    send_sem,
    recv_sem,
):
    rows, n_ch = rec_buf.shape
    near = near_columns(n_grp, n_ch)
    segs = rows // SAMP
    n_recv = n_chan * CH_DEV
    half = n_chan // 2
    me, group = lax.axis_index("chan"), lax.axis_index("grp")
    pair, side = group // 2, group % 2
    first = (1 - side) * half
    want = jnp.where(me < half, 1, 0)
    keeps = side == want
    source_grp = pair * 2 + want

    def target(slot):
        return (first + slot // 2, pair * 2 + slot % 2)

    loads = [
        pltpu.make_async_copy(src, dst, load_sems.at[i])
        for i, (src, dst) in enumerate(
            [
                (lengths_hbm, lengths_ref),
                (pick_hbm, pick_ref),
                (rec_hbm.at[:, pl.ds(0, near)], rec_buf.at[:, pl.ds(0, near)]),
                (dft_hbm, dft_ref),
                (lag_hbm, lag_ref),
                (rec_hbm.at[:, pl.ds(near, n_ch - near)], rec_buf.at[:, pl.ds(near, n_ch - near)]),
            ]
        )
    ]
    for load in loads:
        load.start()
    small, large, rest = loads[:2], loads[2:5], loads[5]
    barrier = pltpu.get_barrier_semaphore()

    def greet(chan):
        pl.semaphore_signal(
            barrier,
            inc=1,
            device_id=(chan, source_grp),
            device_id_type=pl.DeviceIdType.MESH,
        )

    for hop in range(1, n_chan):
        greet(lax.rem(me + hop, n_chan))
    pl.when(jnp.logical_not(keeps))(lambda: greet(me))

    place = lax.broadcasted_iota(jnp.int32, (n_recv, 1), 0)
    slot_chan, slot_grp = target(place // CH_DEV)
    receivers = (slot_chan * n_grp + slot_grp) * CH_DEV + place % CH_DEV

    def gauge_of(channels, columns):
        apart = lax.broadcasted_iota(jnp.int32, (channels.shape[0], columns), 1) - channels
        return jnp.where(apart == 1, 0.5, jnp.where(apart == -1, -0.5, 0.0)).astype(jnp.bfloat16)

    recv_gauge = gauge_of(receivers, n_ch)

    for copy in small:
        copy.wait()
    line = lax.broadcasted_iota(jnp.int32, (STEPS, 128), 1)
    group_of = line % GROUPS
    lengths, picks = lengths_ref[...], pick_ref[...]
    ends = jnp.zeros((STEPS, 128), jnp.int32)
    starts, finish, spots = ends, ends, ends
    for g in range(GROUPS):
        length = jnp.broadcast_to(lengths[:, g : g + 1], ends.shape)
        pick = jnp.broadcast_to(picks[:, g : g + 1], ends.shape)
        spots = jnp.where(group_of == g, ends + lax.shift_right_logical(length * pick, 16), spots)
        starts = jnp.where(group_of == g, ends, starts)
        ends = ends + length
        finish = jnp.where(group_of == g, ends, finish)
    own_step = lax.broadcasted_iota(jnp.int32, ends.shape, 0) == line // GROUPS

    def in_line(table):
        return jnp.sum(jnp.where(own_step, table, 0), axis=0, keepdims=True)

    starts, finish = in_line(starts)[:, :SRC], in_line(finish)[:, :SRC]
    down = lax.broadcasted_iota(jnp.int32, (SRC, 128), 0)
    along = lax.broadcasted_iota(jnp.int32, (SRC, 128), 1)
    sources = jnp.where(down == along, in_line(spots).astype(jnp.float32), 0.0)
    sources = jnp.sum(sources, axis=1, keepdims=True).astype(jnp.int32)
    member = (starts <= receivers) & (receivers < finish)
    step_of = lax.broadcasted_iota(jnp.int32, (n_recv, SRC), 1) // GROUPS
    lanes = lax.broadcasted_iota(jnp.int32, (1, WINDOW), 1)

    def strain_of(gauge, seg):
        window = rec_buf[pl.ds(window_of(seg), WINDOW), pl.ds(0, gauge.shape[1])]
        return lax.dot_general(
            gauge, window, (((1,), (1,)), ((), ())), preferred_element_type=jnp.float32
        )

    def within(seg, series):
        if seg % 2 == 0:
            tail = jnp.where(lanes[:, LANES:] < SAMP, series[:, LANES:], 0.0)
            return jnp.concatenate([series[:, :LANES], tail], axis=1)
        head = jnp.where(lanes[:, :LANES] >= EDGE, series[:, :LANES], 0.0)
        return jnp.concatenate([head, series[:, LANES:]], axis=1)

    def center_of(seg, strain):
        wide = strain.astype(jnp.bfloat16).astype(jnp.float32)
        mean = jnp.sum(within(seg, wide), axis=1, keepdims=True) * (1.0 / SAMP)
        centered = within(seg, wide - mean)
        mean_square = jnp.sum(centered * centered, axis=1, keepdims=True) * (1.0 / SAMP)
        return centered.astype(jnp.bfloat16), lax.rsqrt(mean_square + 1e-06)

    def spectra_of(strains):
        parts = [center_of(seg, strain) for seg, strain in enumerate(strains)]
        series = jnp.concatenate([part[0] for part in parts], axis=0)
        spec = jnp.dot(series, dft_ref[...], preferred_element_type=jnp.float32)
        specs, count = [], strains[0].shape[0]
        for seg, (_, scale) in enumerate(parts):
            part = spec[seg * count : (seg + 1) * count]
            specs.append((part * scale).astype(jnp.bfloat16))
        return specs

    def correlate(slots, receivers, sources):
        begin, end = slots.start * CH_DEV, slots.stop * CH_DEV
        count = end - begin
        spread = jnp.concatenate(
            [jnp.where(member[begin:end] & (step_of[begin:end] == j), 1.0, 0.0) for j in range(STEPS)],
            axis=0,
        ).astype(jnp.bfloat16)
        crosses = [[0.0, 0.0] for _ in range(STEPS)]
        for receiver, source in zip(receivers, sources):
            source = jnp.dot(spread, source, preferred_element_type=jnp.float32)
            rec_real = receiver[:, :HALF].astype(jnp.float32)
            rec_imag = receiver[:, HALF:].astype(jnp.float32)
            for j in range(STEPS):
                src_real = source[j * count : (j + 1) * count, :HALF]
                src_imag = source[j * count : (j + 1) * count, HALF:]
                crosses[j][0] += src_real * rec_real + src_imag * rec_imag
                crosses[j][1] += src_real * rec_imag - src_imag * rec_real
        cross = [jnp.concatenate(parts, axis=1).astype(jnp.bfloat16) for parts in crosses]
        lagged = jnp.dot(
            jnp.concatenate(cross, axis=0), lag_ref[...], preferred_element_type=jnp.float32
        ).astype(jnp.bfloat16)
        return [
            lagged[j * count : (j + 1) * count].reshape(len(slots), CH_DEV, LAGS)
            for j in range(STEPS)
        ]

    own = jnp.where(keeps, 2 * (me - first) + side, n_chan)
    far = jnp.where(me < n_chan - FAR, 0, 1)

    def send(slot):
        return pltpu.make_async_remote_copy(
            src_ref=send_buf.at[slot],
            dst_ref=recv_buf.at[me],
            send_sem=send_sem,
            recv_sem=recv_sem.at[far],
            device_id=target(slot),
            device_id_type=pl.DeviceIdType.MESH,
        )

    def hand_out(slots):
        for slot in slots:
            pl.when(own != slot)(lambda: send(slot).start())
        pl.when((own >= slots.start) & (own < slots.stop))(
            lambda: pltpu.make_async_copy(send_buf.at[own], recv_buf.at[me], recv_sem.at[far]).start()
        )

    early, late = range(EARLY), range(EARLY, n_chan)
    split = EARLY * CH_DEV
    for load in large:
        load.wait()

    def go_early():
        front = jnp.concatenate(
            [recv_gauge[:split, :near], gauge_of(sources, near)], axis=0
        )
        specs = spectra_of([strain_of(front, seg) for seg in range(segs)])
        blocks = correlate(early, [spec[:split] for spec in specs], [spec[split:] for spec in specs])
        for j, block in enumerate(blocks):
            send_buf[pl.ds(0, EARLY), j] = block
        enter()
        hand_out(early)

    def enter():
        pl.semaphore_wait(barrier, jnp.where(keeps, n_chan - 1, n_chan))

    pl.when(side == 1)(go_early)
    rest.wait()
    whole = jnp.concatenate([recv_gauge, gauge_of(sources, n_ch)], axis=0)
    specs = spectra_of([strain_of(whole, seg) for seg in range(segs)])
    blocks = correlate(
        range(n_chan), [spec[:n_recv] for spec in specs], [spec[n_recv:] for spec in specs]
    )
    for j, block in enumerate(blocks):
        send_buf[pl.ds(EARLY, n_chan - EARLY), j] = block[EARLY:]

    def go_late():
        for j, block in enumerate(blocks):
            send_buf[pl.ds(0, EARLY), j] = block[:EARLY]
        enter()
        hand_out(early)

    pl.when(side == 0)(go_late)
    hand_out(late)

    total = 0.0
    for k, chans in enumerate((pl.ds(0, n_chan - FAR), pl.ds(n_chan - FAR, FAR))):
        blocks = recv_buf.at[chans]
        pltpu.make_async_copy(blocks, blocks, recv_sem.at[k]).wait()
        total += jnp.sum(blocks[...].astype(jnp.float32), axis=0)
    mean_square = jnp.sum(total * total, axis=-1, keepdims=True) * (1.0 / LAGS)
    out_ref[...] = total * lax.rsqrt(mean_square + 1e-06)
    most = send_buf.at[pl.ds(0, n_chan - 1)]
    pltpu.make_async_copy(most, most, send_sem).wait()
    pl.when(jnp.logical_not(keeps))(
        lambda: pltpu.make_async_copy(send_buf.at[0], send_buf.at[0], send_sem).wait()
    )


def segment_shards(n_chan, n_grp, record, group_lengths, source_pick):
    rows, n_ch = record.shape
    dft = jnp.asarray(dft_rows(), jnp.bfloat16)
    lag = jnp.asarray(lag_rows(), jnp.bfloat16)
    operands = (record, group_lengths, source_pick, dft, lag)
    block = (STEPS, CH_DEV, LAGS)
    return pl.pallas_call(
        functools.partial(partial_kernel, n_chan, n_grp),
        out_shape=jax.ShapeDtypeStruct(block, jnp.float32),
        in_specs=[pl.BlockSpec(memory_space=pltpu.HBM)] * 5,
        out_specs=pl.BlockSpec(memory_space=pltpu.VMEM),
        scratch_shapes=[
            pltpu.VMEM((STEPS, GROUPS), jnp.int32),
            pltpu.VMEM((STEPS, GROUPS), jnp.int32),
            pltpu.VMEM((rows, n_ch), jnp.bfloat16),
            pltpu.VMEM(dft.shape, jnp.bfloat16),
            pltpu.VMEM(lag.shape, jnp.bfloat16),
            pltpu.VMEM((n_chan,) + block, jnp.bfloat16),
            pltpu.VMEM((n_chan,) + block, jnp.bfloat16),
            pltpu.SemaphoreType.DMA((6,)),
            pltpu.SemaphoreType.DMA,
            pltpu.SemaphoreType.DMA((2,)),
        ],
        compiler_params=pltpu.CompilerParams(
            collective_id=0, has_side_effects=True, vmem_limit_bytes=32 * 1024 * 1024
        ),
    )(*(pltpu.with_memory_space_constraint(x, pltpu.HBM) for x in operands))


def solution(mesh):
    n_chan, n_grp = mesh.shape["chan"], mesh.shape["grp"]

    def local(record, group_lengths, source_pick):
        rows, n_ch = record.shape
        wide = near_columns(n_grp, n_ch) < n_ch
        if rows % (2 * SAMP) == 0 and n_chan * CH_DEV % 128 == 0 and n_grp % 2 == 0 and wide:
            return segment_shards(n_chan, n_grp, record, group_lengths, source_pick)
        return shards(record, group_lengths, source_pick)

    return jax.shard_map(
        local,
        mesh=mesh,
        in_specs=(P("chan", None), P(), P()),
        out_specs=P(None, ("chan", "grp"), None),
        check_vma=False,
    )
```

```python
import functools
import math

import jax
import jax.numpy as jnp
import numpy as np
from jax import lax
from jax.experimental import pallas as pl
from jax.experimental.pallas import tpu as pltpu
from jax.sharding import PartitionSpec as P

CH_DEV = 16
SEG = 32
SAMP = 200
LAGS = 128
STEPS = 4
GROUPS = 16
BINS = 101


def extended(array, sides, width):
    for axis, dim in sides:
        count, length = (lax.axis_size(axis), array.shape[dim])
        up = [(i, (i + 1) % count) for i in range(count - 1)]
        down = [(j, i) for i, j in up]
        last = lax.slice_in_dim(array, length - width, length, axis=dim)
        first = lax.slice_in_dim(array, 0, width, axis=dim)
        before = lax.ppermute(last, axis, up)
        after = lax.ppermute(first, axis, down)
        array = jnp.concatenate([before, array, after], axis=dim)
    return array


def dft_table(samples_count, bins_count):
    samples = jnp.arange(samples_count, dtype=jnp.int32)[:, None]
    freqs = jnp.arange(2 * bins_count, dtype=jnp.int32)[None, :]
    folded = jnp.where(freqs < bins_count, freqs, freqs - bins_count)
    phase = (samples * folded % samples_count).astype(jnp.float32) * (2.0 * math.pi / samples_count)
    return jnp.where(freqs < bins_count, jnp.cos(phase), -jnp.sin(phase)).astype(jnp.bfloat16)


def lag_table(samples_count, bins_count, lag_count):
    freq_rows = jnp.arange(2 * bins_count, dtype=jnp.int32)[:, None]
    lag_cols = jnp.arange(lag_count, dtype=jnp.int32)[None, :] - lag_count // 2
    folded = jnp.where(freq_rows < bins_count, freq_rows, freq_rows - bins_count)
    phase = (folded * lag_cols % samples_count).astype(jnp.float32) * (
        2.0 * math.pi / samples_count
    )
    weights = jnp.where((folded == 0) | (folded == samples_count // 2), 1.0, 2.0).astype(
        jnp.float32
    )
    return weights * jnp.where(freq_rows < bins_count, jnp.cos(phase), -jnp.sin(phase))


def whiten(strain):
    values = strain.astype(jnp.float32).reshape(SEG, SAMP, strain.shape[1])
    means = jnp.mean(values, axis=1, keepdims=True)
    centered = values - means
    mean_square = jnp.mean(centered * centered, axis=1, keepdims=True)
    return (centered / jnp.sqrt(mean_square + 1e-06)).astype(jnp.bfloat16)


def spectral(left, right):
    return jnp.einsum("ksf,sfc->fkc", left, right, preferred_element_type=jnp.float32)


def shards(record, group_lengths, source_pick):
    group_rank = lax.axis_index("grp")
    columns = lax.all_to_all(record, "chan", split_axis=1, concat_axis=0, tiled=True)
    mine = lax.dynamic_slice_in_dim(columns, group_rank * CH_DEV, CH_DEV, 1)
    padded = extended(mine, ((("chan", "grp"), 1),), 1)
    window = padded.astype(jnp.float32)
    strain = ((window[:, 2:] - window[:, :-2]) * 0.5).astype(jnp.bfloat16)
    whitened = whiten(strain)
    spectra = jnp.einsum(
        "snc,nk->skc", whitened, dft_table(SAMP, BINS), preferred_element_type=jnp.float32
    ).astype(jnp.bfloat16)
    first_channel = lax.axis_index(("chan", "grp")) * CH_DEV
    order = jnp.arange(GROUPS, dtype=jnp.int32)
    up_to = order[None, :] <= order[:, None]
    finish = jnp.sum(jnp.where(up_to[None], group_lengths[:, None, :], 0), axis=2)
    starts = finish - group_lengths
    source = starts + group_lengths * source_pick // 65536
    channels = first_channel + jnp.arange(CH_DEV, dtype=jnp.int32)
    owned = (source.reshape(1, -1) == channels[:, None]).astype(jnp.bfloat16)
    partial_table = jnp.einsum("skc,cj->skj", spectra, owned, preferred_element_type=jnp.float32)
    summed = lax.psum(partial_table, ("chan", "grp"))
    source_spec = jnp.transpose(summed.astype(jnp.bfloat16), (2, 0, 1))
    source_spec = source_spec.reshape(STEPS, GROUPS, SEG, 2 * BINS)
    lagt = lag_table(SAMP, BINS, LAGS)
    rec_real = spectra[:, :BINS]
    rec_imag = spectra[:, BINS:]
    traces = []
    for step_index in range(STEPS):
        source_now = source_spec[step_index]
        src_real = source_now[..., :BINS]
        src_imag = source_now[..., BINS:]
        real_all = spectral(src_real, rec_real) + spectral(src_imag, rec_imag)
        imag_all = spectral(src_real, rec_imag) - spectral(src_imag, rec_real)
        members = (
            (channels[None, :] >= starts[step_index][:, None])
            & (channels[None, :] < finish[step_index][:, None])
        ).astype(jnp.float32)
        cross_real = jnp.sum(real_all * members[None], axis=1)
        cross_imag = jnp.sum(imag_all * members[None], axis=1)
        cross_spectrum = jnp.concatenate([cross_real, cross_imag], axis=0)
        lagged = jnp.dot(
            cross_spectrum.T,
            lagt,
            precision=lax.Precision.HIGHEST,
            preferred_element_type=jnp.float32,
        )
        inverse_rms = 1.0 / jnp.sqrt(jnp.mean(lagged * lagged, axis=1, keepdims=True) + 1e-06)
        traces.append(lagged * inverse_rms)
    return jnp.stack(traces)


HALF = 128
LANES = 128
SRC = STEPS * GROUPS
WINDOW = 208
EDGE = WINDOW - SAMP
FAR = 2
EARLY = 2


def turns(rows, columns):
    phase = rows[:, None] * columns[None, :] % SAMP * (2.0 * math.pi / SAMP)
    pad = ((0, 0), (0, HALF - BINS)) if columns.size == BINS else ((0, HALF - BINS), (0, 0))
    return np.pad(np.cos(phase), pad), np.pad(-np.sin(phase), pad)


def dft_rows():
    return np.concatenate(turns(np.arange(WINDOW), np.arange(BINS)), axis=1)


def lag_rows():
    freqs = np.arange(BINS)
    weights = np.where((freqs == 0) | (freqs == SAMP // 2), 1.0, 2.0)
    weights = np.pad(weights, (0, HALF - BINS))[:, None]
    tables = turns(freqs, np.arange(LAGS) - LAGS // 2)
    return np.concatenate([weights * table for table in tables], axis=0)


def near_columns(n_grp, n_ch):
    return -(-(n_grp * CH_DEV + n_ch // 16 + 1) // LANES) * LANES


def window_of(seg):
    return seg * SAMP - seg % 2 * EDGE


def partial_kernel(
    n_chan,
    n_grp,
    rec_hbm,
    lengths_hbm,
    pick_hbm,
    dft_hbm,
    lag_hbm,
    out_ref,
    lengths_ref,
    pick_ref,
    rec_buf,
    dft_ref,
    lag_ref,
    send_buf,
    recv_buf,
    load_sems,
    send_sem,
    recv_sem,
):
    rows, n_ch = rec_buf.shape
    near = near_columns(n_grp, n_ch)
    segs = rows // SAMP
    n_recv = n_chan * CH_DEV
    half = n_chan // 2
    me, group = lax.axis_index("chan"), lax.axis_index("grp")
    pair, side = group // 2, group % 2
    first = (1 - side) * half
    want = jnp.where(me < half, 1, 0)
    keeps = side == want
    source_grp = pair * 2 + want

    def target(slot):
        return (first + slot // 2, pair * 2 + slot % 2)

    loads = [
        pltpu.make_async_copy(src, dst, load_sems.at[i])
        for i, (src, dst) in enumerate(
            [
                (lengths_hbm, lengths_ref),
                (pick_hbm, pick_ref),
                (rec_hbm.at[:, pl.ds(0, near)], rec_buf.at[:, pl.ds(0, near)]),
                (dft_hbm, dft_ref),
                (lag_hbm, lag_ref),
                (rec_hbm.at[:, pl.ds(near, n_ch - near)], rec_buf.at[:, pl.ds(near, n_ch - near)]),
            ]
        )
    ]
    for load in loads:
        load.start()
    small, large, rest = loads[:2], loads[2:5], loads[5]
    barrier = pltpu.get_barrier_semaphore()

    def greet(chan):
        pl.semaphore_signal(
            barrier,
            inc=1,
            device_id=(chan, source_grp),
            device_id_type=pl.DeviceIdType.MESH,
        )

    for hop in range(1, n_chan):
        greet(lax.rem(me + hop, n_chan))
    pl.when(jnp.logical_not(keeps))(lambda: greet(me))

    place = lax.broadcasted_iota(jnp.int32, (n_recv, 1), 0)
    slot_chan, slot_grp = target(place // CH_DEV)
    receivers = (slot_chan * n_grp + slot_grp) * CH_DEV + place % CH_DEV

    def gauge_of(channels, columns):
        apart = lax.broadcasted_iota(jnp.int32, (channels.shape[0], columns), 1) - channels
        return jnp.where(apart == 1, 0.5, jnp.where(apart == -1, -0.5, 0.0)).astype(jnp.bfloat16)

    recv_gauge = gauge_of(receivers, n_ch)

    for copy in small:
        copy.wait()
    line = lax.broadcasted_iota(jnp.int32, (STEPS, 128), 1)
    group_of = line % GROUPS
    lengths, picks = lengths_ref[...], pick_ref[...]
    ends = jnp.zeros((STEPS, 128), jnp.int32)
    starts, finish, spots = ends, ends, ends
    for g in range(GROUPS):
        length = jnp.broadcast_to(lengths[:, g : g + 1], ends.shape)
        pick = jnp.broadcast_to(picks[:, g : g + 1], ends.shape)
        spots = jnp.where(group_of == g, ends + lax.shift_right_logical(length * pick, 16), spots)
        starts = jnp.where(group_of == g, ends, starts)
        ends = ends + length
        finish = jnp.where(group_of == g, ends, finish)
    own_step = lax.broadcasted_iota(jnp.int32, ends.shape, 0) == line // GROUPS

    def in_line(table):
        return jnp.sum(jnp.where(own_step, table, 0), axis=0, keepdims=True)

    starts, finish = in_line(starts)[:, :SRC], in_line(finish)[:, :SRC]
    down = lax.broadcasted_iota(jnp.int32, (SRC, 128), 0)
    along = lax.broadcasted_iota(jnp.int32, (SRC, 128), 1)
    sources = jnp.where(down == along, in_line(spots).astype(jnp.float32), 0.0)
    sources = jnp.sum(sources, axis=1, keepdims=True).astype(jnp.int32)
    member = (starts <= receivers) & (receivers < finish)
    step_of = lax.broadcasted_iota(jnp.int32, (n_recv, SRC), 1) // GROUPS
    lanes = lax.broadcasted_iota(jnp.int32, (1, WINDOW), 1)

    def strain_of(gauge, seg):
        window = rec_buf[pl.ds(window_of(seg), WINDOW), pl.ds(0, gauge.shape[1])]
        return lax.dot_general(
            gauge, window, (((1,), (1,)), ((), ())), preferred_element_type=jnp.float32
        )

    def within(seg, series):
        if seg % 2 == 0:
            tail = jnp.where(lanes[:, LANES:] < SAMP, series[:, LANES:], 0.0)
            return jnp.concatenate([series[:, :LANES], tail], axis=1)
        head = jnp.where(lanes[:, :LANES] >= EDGE, series[:, :LANES], 0.0)
        return jnp.concatenate([head, series[:, LANES:]], axis=1)

    def center_of(seg, strain):
        wide = strain.astype(jnp.bfloat16).astype(jnp.float32)
        mean = jnp.sum(within(seg, wide), axis=1, keepdims=True) * (1.0 / SAMP)
        centered = within(seg, wide - mean)
        mean_square = jnp.sum(centered * centered, axis=1, keepdims=True) * (1.0 / SAMP)
        return centered.astype(jnp.bfloat16), lax.rsqrt(mean_square + 1e-06)

    def spectra_of(strains):
        parts = [center_of(seg, strain) for seg, strain in enumerate(strains)]
        series = jnp.concatenate([part[0] for part in parts], axis=0)
        spec = jnp.dot(series, dft_ref[...], preferred_element_type=jnp.float32)
        specs, count = [], strains[0].shape[0]
        for seg, (_, scale) in enumerate(parts):
            part = spec[seg * count : (seg + 1) * count]
            specs.append((part * scale).astype(jnp.bfloat16))
        return specs

    def correlate(slots, receivers, sources):
        begin, end = slots.start * CH_DEV, slots.stop * CH_DEV
        count = end - begin
        spread = jnp.concatenate(
            [jnp.where(member[begin:end] & (step_of[begin:end] == j), 1.0, 0.0) for j in range(STEPS)],
            axis=0,
        ).astype(jnp.bfloat16)
        crosses = [[0.0, 0.0] for _ in range(STEPS)]
        for receiver, source in zip(receivers, sources):
            source = jnp.dot(spread, source, preferred_element_type=jnp.float32)
            rec_real = receiver[:, :HALF].astype(jnp.float32)
            rec_imag = receiver[:, HALF:].astype(jnp.float32)
            for j in range(STEPS):
                src_real = source[j * count : (j + 1) * count, :HALF]
                src_imag = source[j * count : (j + 1) * count, HALF:]
                crosses[j][0] += src_real * rec_real + src_imag * rec_imag
                crosses[j][1] += src_real * rec_imag - src_imag * rec_real
        cross = [jnp.concatenate(parts, axis=1).astype(jnp.bfloat16) for parts in crosses]
        lagged = jnp.dot(
            jnp.concatenate(cross, axis=0), lag_ref[...], preferred_element_type=jnp.float32
        ).astype(jnp.bfloat16)
        return [
            lagged[j * count : (j + 1) * count].reshape(len(slots), CH_DEV, LAGS)
            for j in range(STEPS)
        ]

    own = jnp.where(keeps, 2 * (me - first) + side, n_chan)
    far = jnp.where(me < n_chan - FAR, 0, 1)

    def send(slot):
        return pltpu.make_async_remote_copy(
            src_ref=send_buf.at[slot],
            dst_ref=recv_buf.at[me],
            send_sem=send_sem,
            recv_sem=recv_sem.at[far],
            device_id=target(slot),
            device_id_type=pl.DeviceIdType.MESH,
        )

    def hand_out(slots):
        for slot in slots:
            pl.when(own != slot)(lambda: send(slot).start())
        pl.when((own >= slots.start) & (own < slots.stop))(
            lambda: pltpu.make_async_copy(send_buf.at[own], recv_buf.at[me], recv_sem.at[far]).start()
        )

    early, late = range(EARLY), range(EARLY, n_chan)
    split = EARLY * CH_DEV
    for load in large:
        load.wait()

    def go_early():
        front = jnp.concatenate(
            [recv_gauge[:split, :near], gauge_of(sources, near)], axis=0
        )
        specs = spectra_of([strain_of(front, seg) for seg in range(segs)])
        blocks = correlate(early, [spec[:split] for spec in specs], [spec[split:] for spec in specs])
        for j, block in enumerate(blocks):
            send_buf[pl.ds(0, EARLY), j] = block
        enter()
        hand_out(early)

    def enter():
        pl.semaphore_wait(barrier, jnp.where(keeps, n_chan - 1, n_chan))

    def finish_with(slots):
        rest.wait()
        skip = slots.start * CH_DEV
        whole = jnp.concatenate([recv_gauge[skip:], gauge_of(sources, n_ch)], axis=0)
        specs = spectra_of([strain_of(whole, seg) for seg in range(segs)])
        held = n_recv - skip
        blocks = correlate(slots, [spec[:held] for spec in specs], [spec[held:] for spec in specs])
        for j, block in enumerate(blocks):
            send_buf[pl.ds(slots.start, len(slots)), j] = block

    @pl.when(side == 1)
    def _():
        go_early()
        finish_with(late)
        hand_out(late)

    @pl.when(side == 0)
    def _():
        finish_with(range(n_chan))
        enter()
        hand_out(range(n_chan))

    total = 0.0
    for k, chans in enumerate((pl.ds(0, n_chan - FAR), pl.ds(n_chan - FAR, FAR))):
        blocks = recv_buf.at[chans]
        pltpu.make_async_copy(blocks, blocks, recv_sem.at[k]).wait()
        total += jnp.sum(blocks[...].astype(jnp.float32), axis=0)
    mean_square = jnp.sum(total * total, axis=-1, keepdims=True) * (1.0 / LAGS)
    out_ref[...] = total * lax.rsqrt(mean_square + 1e-06)
    most = send_buf.at[pl.ds(0, n_chan - 1)]
    pltpu.make_async_copy(most, most, send_sem).wait()
    pl.when(jnp.logical_not(keeps))(
        lambda: pltpu.make_async_copy(send_buf.at[0], send_buf.at[0], send_sem).wait()
    )


def segment_shards(n_chan, n_grp, record, group_lengths, source_pick):
    rows, n_ch = record.shape
    dft = jnp.asarray(dft_rows(), jnp.bfloat16)
    lag = jnp.asarray(lag_rows(), jnp.bfloat16)
    operands = (record, group_lengths, source_pick, dft, lag)
    block = (STEPS, CH_DEV, LAGS)
    return pl.pallas_call(
        functools.partial(partial_kernel, n_chan, n_grp),
        out_shape=jax.ShapeDtypeStruct(block, jnp.float32),
        in_specs=[pl.BlockSpec(memory_space=pltpu.HBM)] * 5,
        out_specs=pl.BlockSpec(memory_space=pltpu.VMEM),
        scratch_shapes=[
            pltpu.VMEM((STEPS, GROUPS), jnp.int32),
            pltpu.VMEM((STEPS, GROUPS), jnp.int32),
            pltpu.VMEM((rows, n_ch), jnp.bfloat16),
            pltpu.VMEM(dft.shape, jnp.bfloat16),
            pltpu.VMEM(lag.shape, jnp.bfloat16),
            pltpu.VMEM((n_chan,) + block, jnp.bfloat16),
            pltpu.VMEM((n_chan,) + block, jnp.bfloat16),
            pltpu.SemaphoreType.DMA((6,)),
            pltpu.SemaphoreType.DMA,
            pltpu.SemaphoreType.DMA((2,)),
        ],
        compiler_params=pltpu.CompilerParams(
            collective_id=0, has_side_effects=True, vmem_limit_bytes=32 * 1024 * 1024
        ),
    )(*(pltpu.with_memory_space_constraint(x, pltpu.HBM) for x in operands))


def solution(mesh):
    n_chan, n_grp = mesh.shape["chan"], mesh.shape["grp"]

    def local(record, group_lengths, source_pick):
        rows, n_ch = record.shape
        wide = near_columns(n_grp, n_ch) < n_ch
        if rows % (2 * SAMP) == 0 and n_chan * CH_DEV % 128 == 0 and n_grp % 2 == 0 and wide:
            return segment_shards(n_chan, n_grp, record, group_lengths, source_pick)
        return shards(record, group_lengths, source_pick)

    return jax.shard_map(
        local,
        mesh=mesh,
        in_specs=(P("chan", None), P(), P()),
        out_specs=P(None, ("chan", "grp"), None),
        check_vma=False,
    )
```

```python
import functools
import math

import jax
import jax.numpy as jnp
import numpy as np
from jax import lax
from jax.experimental import pallas as pl
from jax.experimental.pallas import tpu as pltpu
from jax.sharding import PartitionSpec as P

CH_DEV = 16
SEG = 32
SAMP = 200
LAGS = 128
STEPS = 4
GROUPS = 16
BINS = 101


def extended(array, sides, width):
    for axis, dim in sides:
        count, length = (lax.axis_size(axis), array.shape[dim])
        up = [(i, (i + 1) % count) for i in range(count - 1)]
        down = [(j, i) for i, j in up]
        last = lax.slice_in_dim(array, length - width, length, axis=dim)
        first = lax.slice_in_dim(array, 0, width, axis=dim)
        before = lax.ppermute(last, axis, up)
        after = lax.ppermute(first, axis, down)
        array = jnp.concatenate([before, array, after], axis=dim)
    return array


def dft_table(samples_count, bins_count):
    samples = jnp.arange(samples_count, dtype=jnp.int32)[:, None]
    freqs = jnp.arange(2 * bins_count, dtype=jnp.int32)[None, :]
    folded = jnp.where(freqs < bins_count, freqs, freqs - bins_count)
    phase = (samples * folded % samples_count).astype(jnp.float32) * (2.0 * math.pi / samples_count)
    return jnp.where(freqs < bins_count, jnp.cos(phase), -jnp.sin(phase)).astype(jnp.bfloat16)


def lag_table(samples_count, bins_count, lag_count):
    freq_rows = jnp.arange(2 * bins_count, dtype=jnp.int32)[:, None]
    lag_cols = jnp.arange(lag_count, dtype=jnp.int32)[None, :] - lag_count // 2
    folded = jnp.where(freq_rows < bins_count, freq_rows, freq_rows - bins_count)
    phase = (folded * lag_cols % samples_count).astype(jnp.float32) * (
        2.0 * math.pi / samples_count
    )
    weights = jnp.where((folded == 0) | (folded == samples_count // 2), 1.0, 2.0).astype(
        jnp.float32
    )
    return weights * jnp.where(freq_rows < bins_count, jnp.cos(phase), -jnp.sin(phase))


def whiten(strain):
    values = strain.astype(jnp.float32).reshape(SEG, SAMP, strain.shape[1])
    means = jnp.mean(values, axis=1, keepdims=True)
    centered = values - means
    mean_square = jnp.mean(centered * centered, axis=1, keepdims=True)
    return (centered / jnp.sqrt(mean_square + 1e-06)).astype(jnp.bfloat16)


def spectral(left, right):
    return jnp.einsum("ksf,sfc->fkc", left, right, preferred_element_type=jnp.float32)


def shards(record, group_lengths, source_pick):
    group_rank = lax.axis_index("grp")
    columns = lax.all_to_all(record, "chan", split_axis=1, concat_axis=0, tiled=True)
    mine = lax.dynamic_slice_in_dim(columns, group_rank * CH_DEV, CH_DEV, 1)
    padded = extended(mine, ((("chan", "grp"), 1),), 1)
    window = padded.astype(jnp.float32)
    strain = ((window[:, 2:] - window[:, :-2]) * 0.5).astype(jnp.bfloat16)
    whitened = whiten(strain)
    spectra = jnp.einsum(
        "snc,nk->skc", whitened, dft_table(SAMP, BINS), preferred_element_type=jnp.float32
    ).astype(jnp.bfloat16)
    first_channel = lax.axis_index(("chan", "grp")) * CH_DEV
    order = jnp.arange(GROUPS, dtype=jnp.int32)
    up_to = order[None, :] <= order[:, None]
    finish = jnp.sum(jnp.where(up_to[None], group_lengths[:, None, :], 0), axis=2)
    starts = finish - group_lengths
    source = starts + group_lengths * source_pick // 65536
    channels = first_channel + jnp.arange(CH_DEV, dtype=jnp.int32)
    owned = (source.reshape(1, -1) == channels[:, None]).astype(jnp.bfloat16)
    partial_table = jnp.einsum("skc,cj->skj", spectra, owned, preferred_element_type=jnp.float32)
    summed = lax.psum(partial_table, ("chan", "grp"))
    source_spec = jnp.transpose(summed.astype(jnp.bfloat16), (2, 0, 1))
    source_spec = source_spec.reshape(STEPS, GROUPS, SEG, 2 * BINS)
    lagt = lag_table(SAMP, BINS, LAGS)
    rec_real = spectra[:, :BINS]
    rec_imag = spectra[:, BINS:]
    traces = []
    for step_index in range(STEPS):
        source_now = source_spec[step_index]
        src_real = source_now[..., :BINS]
        src_imag = source_now[..., BINS:]
        real_all = spectral(src_real, rec_real) + spectral(src_imag, rec_imag)
        imag_all = spectral(src_real, rec_imag) - spectral(src_imag, rec_real)
        members = (
            (channels[None, :] >= starts[step_index][:, None])
            & (channels[None, :] < finish[step_index][:, None])
        ).astype(jnp.float32)
        cross_real = jnp.sum(real_all * members[None], axis=1)
        cross_imag = jnp.sum(imag_all * members[None], axis=1)
        cross_spectrum = jnp.concatenate([cross_real, cross_imag], axis=0)
        lagged = jnp.dot(
            cross_spectrum.T,
            lagt,
            precision=lax.Precision.HIGHEST,
            preferred_element_type=jnp.float32,
        )
        inverse_rms = 1.0 / jnp.sqrt(jnp.mean(lagged * lagged, axis=1, keepdims=True) + 1e-06)
        traces.append(lagged * inverse_rms)
    return jnp.stack(traces)


HALF = 128
LANES = 128
SRC = STEPS * GROUPS
WINDOW = 208
EDGE = WINDOW - SAMP
FAR = 1
EARLY = 2


def turns(rows, columns):
    phase = rows[:, None] * columns[None, :] % SAMP * (2.0 * math.pi / SAMP)
    pad = ((0, 0), (0, HALF - BINS)) if columns.size == BINS else ((0, HALF - BINS), (0, 0))
    return np.pad(np.cos(phase), pad), np.pad(-np.sin(phase), pad)


def dft_rows():
    return np.concatenate(turns(np.arange(WINDOW), np.arange(BINS)), axis=1)


def lag_rows():
    freqs = np.arange(BINS)
    weights = np.where((freqs == 0) | (freqs == SAMP // 2), 1.0, 2.0)
    weights = np.pad(weights, (0, HALF - BINS))[:, None]
    tables = turns(freqs, np.arange(LAGS) - LAGS // 2)
    return np.concatenate([weights * table for table in tables], axis=0)


def near_columns(n_grp, n_ch):
    return -(-(n_grp * CH_DEV + n_ch // 16 + 1) // LANES) * LANES


def window_of(seg):
    return seg * SAMP - seg % 2 * EDGE


def partial_kernel(
    n_chan,
    n_grp,
    rec_hbm,
    lengths_hbm,
    pick_hbm,
    dft_hbm,
    lag_hbm,
    out_ref,
    lengths_ref,
    pick_ref,
    rec_buf,
    dft_ref,
    lag_ref,
    send_buf,
    recv_buf,
    load_sems,
    send_sem,
    recv_sem,
):
    rows, n_ch = rec_buf.shape
    near = near_columns(n_grp, n_ch)
    segs = rows // SAMP
    n_recv = n_chan * CH_DEV
    half = n_chan // 2
    me, group = lax.axis_index("chan"), lax.axis_index("grp")
    pair, side = group // 2, group % 2
    first = (1 - side) * half
    want = jnp.where(me < half, 1, 0)
    keeps = side == want
    source_grp = pair * 2 + want

    def target(slot):
        return (first + slot // 2, pair * 2 + slot % 2)

    loads = [
        pltpu.make_async_copy(src, dst, load_sems.at[i])
        for i, (src, dst) in enumerate(
            [
                (lengths_hbm, lengths_ref),
                (pick_hbm, pick_ref),
                (rec_hbm.at[:, pl.ds(0, near)], rec_buf.at[:, pl.ds(0, near)]),
                (dft_hbm, dft_ref),
                (lag_hbm, lag_ref),
                (rec_hbm.at[:, pl.ds(near, n_ch - near)], rec_buf.at[:, pl.ds(near, n_ch - near)]),
            ]
        )
    ]
    for load in loads:
        load.start()
    small, large, rest = loads[:2], loads[2:5], loads[5]
    barrier = pltpu.get_barrier_semaphore()

    def greet(chan):
        pl.semaphore_signal(
            barrier,
            inc=1,
            device_id=(chan, source_grp),
            device_id_type=pl.DeviceIdType.MESH,
        )

    for hop in range(1, n_chan):
        greet(lax.rem(me + hop, n_chan))
    pl.when(jnp.logical_not(keeps))(lambda: greet(me))

    place = lax.broadcasted_iota(jnp.int32, (n_recv, 1), 0)
    slot_chan, slot_grp = target(place // CH_DEV)
    receivers = (slot_chan * n_grp + slot_grp) * CH_DEV + place % CH_DEV

    def gauge_of(channels, columns):
        apart = lax.broadcasted_iota(jnp.int32, (channels.shape[0], columns), 1) - channels
        return jnp.where(apart == 1, 0.5, jnp.where(apart == -1, -0.5, 0.0)).astype(jnp.bfloat16)

    recv_gauge = gauge_of(receivers, n_ch)

    for copy in small:
        copy.wait()
    line = lax.broadcasted_iota(jnp.int32, (STEPS, 128), 1)
    group_of = line % GROUPS
    lengths, picks = lengths_ref[...], pick_ref[...]
    ends = jnp.zeros((STEPS, 128), jnp.int32)
    starts, finish, spots = ends, ends, ends
    for g in range(GROUPS):
        length = jnp.broadcast_to(lengths[:, g : g + 1], ends.shape)
        pick = jnp.broadcast_to(picks[:, g : g + 1], ends.shape)
        spots = jnp.where(group_of == g, ends + lax.shift_right_logical(length * pick, 16), spots)
        starts = jnp.where(group_of == g, ends, starts)
        ends = ends + length
        finish = jnp.where(group_of == g, ends, finish)
    own_step = lax.broadcasted_iota(jnp.int32, ends.shape, 0) == line // GROUPS

    def in_line(table):
        return jnp.sum(jnp.where(own_step, table, 0), axis=0, keepdims=True)

    starts, finish = in_line(starts)[:, :SRC], in_line(finish)[:, :SRC]
    down = lax.broadcasted_iota(jnp.int32, (SRC, 128), 0)
    along = lax.broadcasted_iota(jnp.int32, (SRC, 128), 1)
    sources = jnp.where(down == along, in_line(spots).astype(jnp.float32), 0.0)
    sources = jnp.sum(sources, axis=1, keepdims=True).astype(jnp.int32)
    member = (starts <= receivers) & (receivers < finish)
    step_of = lax.broadcasted_iota(jnp.int32, (n_recv, SRC), 1) // GROUPS
    lanes = lax.broadcasted_iota(jnp.int32, (1, WINDOW), 1)

    def strain_of(gauge, seg):
        window = rec_buf[pl.ds(window_of(seg), WINDOW), pl.ds(0, gauge.shape[1])]
        return lax.dot_general(
            gauge, window, (((1,), (1,)), ((), ())), preferred_element_type=jnp.float32
        )

    def within(seg, series):
        if seg % 2 == 0:
            tail = jnp.where(lanes[:, LANES:] < SAMP, series[:, LANES:], 0.0)
            return jnp.concatenate([series[:, :LANES], tail], axis=1)
        head = jnp.where(lanes[:, :LANES] >= EDGE, series[:, :LANES], 0.0)
        return jnp.concatenate([head, series[:, LANES:]], axis=1)

    def center_of(seg, strain):
        wide = strain.astype(jnp.bfloat16).astype(jnp.float32)
        mean = jnp.sum(within(seg, wide), axis=1, keepdims=True) * (1.0 / SAMP)
        centered = within(seg, wide - mean)
        mean_square = jnp.sum(centered * centered, axis=1, keepdims=True) * (1.0 / SAMP)
        return centered.astype(jnp.bfloat16), lax.rsqrt(mean_square + 1e-06)

    def spectra_of(strains):
        parts = [center_of(seg, strain) for seg, strain in enumerate(strains)]
        series = jnp.concatenate([part[0] for part in parts], axis=0)
        spec = jnp.dot(series, dft_ref[...], preferred_element_type=jnp.float32)
        specs, count = [], strains[0].shape[0]
        for seg, (_, scale) in enumerate(parts):
            part = spec[seg * count : (seg + 1) * count]
            specs.append((part * scale).astype(jnp.bfloat16))
        return specs

    def correlate(slots, receivers, sources):
        begin, end = slots.start * CH_DEV, slots.stop * CH_DEV
        count = end - begin
        spread = jnp.concatenate(
            [jnp.where(member[begin:end] & (step_of[begin:end] == j), 1.0, 0.0) for j in range(STEPS)],
            axis=0,
        ).astype(jnp.bfloat16)
        crosses = [[0.0, 0.0] for _ in range(STEPS)]
        for receiver, source in zip(receivers, sources):
            source = jnp.dot(spread, source, preferred_element_type=jnp.float32)
            rec_real = receiver[:, :HALF].astype(jnp.float32)
            rec_imag = receiver[:, HALF:].astype(jnp.float32)
            for j in range(STEPS):
                src_real = source[j * count : (j + 1) * count, :HALF]
                src_imag = source[j * count : (j + 1) * count, HALF:]
                crosses[j][0] += src_real * rec_real + src_imag * rec_imag
                crosses[j][1] += src_real * rec_imag - src_imag * rec_real
        cross = [jnp.concatenate(parts, axis=1).astype(jnp.bfloat16) for parts in crosses]
        lagged = jnp.dot(
            jnp.concatenate(cross, axis=0), lag_ref[...], preferred_element_type=jnp.float32
        ).astype(jnp.bfloat16)
        return [
            lagged[j * count : (j + 1) * count].reshape(len(slots), CH_DEV, LAGS)
            for j in range(STEPS)
        ]

    own = jnp.where(keeps, 2 * (me - first) + side, n_chan)
    far = jnp.where(me < n_chan - FAR, 0, 1)

    def send(slot):
        return pltpu.make_async_remote_copy(
            src_ref=send_buf.at[slot],
            dst_ref=recv_buf.at[me],
            send_sem=send_sem,
            recv_sem=recv_sem.at[far],
            device_id=target(slot),
            device_id_type=pl.DeviceIdType.MESH,
        )

    def hand_out(slots):
        for slot in slots:
            pl.when(own != slot)(lambda: send(slot).start())
        pl.when((own >= slots.start) & (own < slots.stop))(
            lambda: pltpu.make_async_copy(send_buf.at[own], recv_buf.at[me], recv_sem.at[far]).start()
        )

    early, late = range(EARLY), range(EARLY, n_chan)
    split = EARLY * CH_DEV
    for load in large:
        load.wait()

    def go_early():
        front = jnp.concatenate(
            [recv_gauge[:split, :near], gauge_of(sources, near)], axis=0
        )
        specs = spectra_of([strain_of(front, seg) for seg in range(segs)])
        blocks = correlate(early, [spec[:split] for spec in specs], [spec[split:] for spec in specs])
        for j, block in enumerate(blocks):
            send_buf[pl.ds(0, EARLY), j] = block
        enter()
        hand_out(early)

    def enter():
        pl.semaphore_wait(barrier, jnp.where(keeps, n_chan - 1, n_chan))

    def finish_with(slots):
        rest.wait()
        skip = slots.start * CH_DEV
        whole = jnp.concatenate([recv_gauge[skip:], gauge_of(sources, n_ch)], axis=0)
        specs = spectra_of([strain_of(whole, seg) for seg in range(segs)])
        held = n_recv - skip
        blocks = correlate(slots, [spec[:held] for spec in specs], [spec[held:] for spec in specs])
        for j, block in enumerate(blocks):
            send_buf[pl.ds(slots.start, len(slots)), j] = block

    @pl.when(side == 1)
    def _():
        go_early()
        finish_with(late)
        hand_out(late)

    @pl.when(side == 0)
    def _():
        finish_with(range(n_chan))
        enter()
        hand_out(range(n_chan))

    total = 0.0
    for k, chans in enumerate((pl.ds(0, n_chan - FAR), pl.ds(n_chan - FAR, FAR))):
        blocks = recv_buf.at[chans]
        pltpu.make_async_copy(blocks, blocks, recv_sem.at[k]).wait()
        total += jnp.sum(blocks[...].astype(jnp.float32), axis=0)
    mean_square = jnp.sum(total * total, axis=-1, keepdims=True) * (1.0 / LAGS)
    out_ref[...] = total * lax.rsqrt(mean_square + 1e-06)
    most = send_buf.at[pl.ds(0, n_chan - 1)]
    pltpu.make_async_copy(most, most, send_sem).wait()
    pl.when(jnp.logical_not(keeps))(
        lambda: pltpu.make_async_copy(send_buf.at[0], send_buf.at[0], send_sem).wait()
    )


def segment_shards(n_chan, n_grp, record, group_lengths, source_pick):
    rows, n_ch = record.shape
    dft = jnp.asarray(dft_rows(), jnp.bfloat16)
    lag = jnp.asarray(lag_rows(), jnp.bfloat16)
    operands = (record, group_lengths, source_pick, dft, lag)
    block = (STEPS, CH_DEV, LAGS)
    return pl.pallas_call(
        functools.partial(partial_kernel, n_chan, n_grp),
        out_shape=jax.ShapeDtypeStruct(block, jnp.float32),
        in_specs=[pl.BlockSpec(memory_space=pltpu.HBM)] * 5,
        out_specs=pl.BlockSpec(memory_space=pltpu.VMEM),
        scratch_shapes=[
            pltpu.VMEM((STEPS, GROUPS), jnp.int32),
            pltpu.VMEM((STEPS, GROUPS), jnp.int32),
            pltpu.VMEM((rows, n_ch), jnp.bfloat16),
            pltpu.VMEM(dft.shape, jnp.bfloat16),
            pltpu.VMEM(lag.shape, jnp.bfloat16),
            pltpu.VMEM((n_chan,) + block, jnp.bfloat16),
            pltpu.VMEM((n_chan,) + block, jnp.bfloat16),
            pltpu.SemaphoreType.DMA((6,)),
            pltpu.SemaphoreType.DMA,
            pltpu.SemaphoreType.DMA((2,)),
        ],
        compiler_params=pltpu.CompilerParams(
            collective_id=0, has_side_effects=True, vmem_limit_bytes=32 * 1024 * 1024
        ),
    )(*(pltpu.with_memory_space_constraint(x, pltpu.HBM) for x in operands))


def solution(mesh):
    n_chan, n_grp = mesh.shape["chan"], mesh.shape["grp"]

    def local(record, group_lengths, source_pick):
        rows, n_ch = record.shape
        wide = near_columns(n_grp, n_ch) < n_ch
        if rows % (2 * SAMP) == 0 and n_chan * CH_DEV % 128 == 0 and n_grp % 2 == 0 and wide:
            return segment_shards(n_chan, n_grp, record, group_lengths, source_pick)
        return shards(record, group_lengths, source_pick)

    return jax.shard_map(
        local,
        mesh=mesh,
        in_specs=(P("chan", None), P(), P()),
        out_specs=P(None, ("chan", "grp"), None),
        check_vma=False,
    )
```

```python
import functools
import math

import jax
import jax.numpy as jnp
import numpy as np
from jax import lax
from jax.experimental import pallas as pl
from jax.experimental.pallas import tpu as pltpu
from jax.sharding import PartitionSpec as P

CH_DEV = 16
SEG = 32
SAMP = 200
LAGS = 128
STEPS = 4
GROUPS = 16
BINS = 101


def extended(array, sides, width):
    for axis, dim in sides:
        count, length = (lax.axis_size(axis), array.shape[dim])
        up = [(i, (i + 1) % count) for i in range(count - 1)]
        down = [(j, i) for i, j in up]
        last = lax.slice_in_dim(array, length - width, length, axis=dim)
        first = lax.slice_in_dim(array, 0, width, axis=dim)
        before = lax.ppermute(last, axis, up)
        after = lax.ppermute(first, axis, down)
        array = jnp.concatenate([before, array, after], axis=dim)
    return array


def dft_table(samples_count, bins_count):
    samples = jnp.arange(samples_count, dtype=jnp.int32)[:, None]
    freqs = jnp.arange(2 * bins_count, dtype=jnp.int32)[None, :]
    folded = jnp.where(freqs < bins_count, freqs, freqs - bins_count)
    phase = (samples * folded % samples_count).astype(jnp.float32) * (2.0 * math.pi / samples_count)
    return jnp.where(freqs < bins_count, jnp.cos(phase), -jnp.sin(phase)).astype(jnp.bfloat16)


def lag_table(samples_count, bins_count, lag_count):
    freq_rows = jnp.arange(2 * bins_count, dtype=jnp.int32)[:, None]
    lag_cols = jnp.arange(lag_count, dtype=jnp.int32)[None, :] - lag_count // 2
    folded = jnp.where(freq_rows < bins_count, freq_rows, freq_rows - bins_count)
    phase = (folded * lag_cols % samples_count).astype(jnp.float32) * (
        2.0 * math.pi / samples_count
    )
    weights = jnp.where((folded == 0) | (folded == samples_count // 2), 1.0, 2.0).astype(
        jnp.float32
    )
    return weights * jnp.where(freq_rows < bins_count, jnp.cos(phase), -jnp.sin(phase))


def whiten(strain):
    values = strain.astype(jnp.float32).reshape(SEG, SAMP, strain.shape[1])
    means = jnp.mean(values, axis=1, keepdims=True)
    centered = values - means
    mean_square = jnp.mean(centered * centered, axis=1, keepdims=True)
    return (centered / jnp.sqrt(mean_square + 1e-06)).astype(jnp.bfloat16)


def spectral(left, right):
    return jnp.einsum("ksf,sfc->fkc", left, right, preferred_element_type=jnp.float32)


def shards(record, group_lengths, source_pick):
    group_rank = lax.axis_index("grp")
    columns = lax.all_to_all(record, "chan", split_axis=1, concat_axis=0, tiled=True)
    mine = lax.dynamic_slice_in_dim(columns, group_rank * CH_DEV, CH_DEV, 1)
    padded = extended(mine, ((("chan", "grp"), 1),), 1)
    window = padded.astype(jnp.float32)
    strain = ((window[:, 2:] - window[:, :-2]) * 0.5).astype(jnp.bfloat16)
    whitened = whiten(strain)
    spectra = jnp.einsum(
        "snc,nk->skc", whitened, dft_table(SAMP, BINS), preferred_element_type=jnp.float32
    ).astype(jnp.bfloat16)
    first_channel = lax.axis_index(("chan", "grp")) * CH_DEV
    order = jnp.arange(GROUPS, dtype=jnp.int32)
    up_to = order[None, :] <= order[:, None]
    finish = jnp.sum(jnp.where(up_to[None], group_lengths[:, None, :], 0), axis=2)
    starts = finish - group_lengths
    source = starts + group_lengths * source_pick // 65536
    channels = first_channel + jnp.arange(CH_DEV, dtype=jnp.int32)
    owned = (source.reshape(1, -1) == channels[:, None]).astype(jnp.bfloat16)
    partial_table = jnp.einsum("skc,cj->skj", spectra, owned, preferred_element_type=jnp.float32)
    summed = lax.psum(partial_table, ("chan", "grp"))
    source_spec = jnp.transpose(summed.astype(jnp.bfloat16), (2, 0, 1))
    source_spec = source_spec.reshape(STEPS, GROUPS, SEG, 2 * BINS)
    lagt = lag_table(SAMP, BINS, LAGS)
    rec_real = spectra[:, :BINS]
    rec_imag = spectra[:, BINS:]
    traces = []
    for step_index in range(STEPS):
        source_now = source_spec[step_index]
        src_real = source_now[..., :BINS]
        src_imag = source_now[..., BINS:]
        real_all = spectral(src_real, rec_real) + spectral(src_imag, rec_imag)
        imag_all = spectral(src_real, rec_imag) - spectral(src_imag, rec_real)
        members = (
            (channels[None, :] >= starts[step_index][:, None])
            & (channels[None, :] < finish[step_index][:, None])
        ).astype(jnp.float32)
        cross_real = jnp.sum(real_all * members[None], axis=1)
        cross_imag = jnp.sum(imag_all * members[None], axis=1)
        cross_spectrum = jnp.concatenate([cross_real, cross_imag], axis=0)
        lagged = jnp.dot(
            cross_spectrum.T,
            lagt,
            precision=lax.Precision.HIGHEST,
            preferred_element_type=jnp.float32,
        )
        inverse_rms = 1.0 / jnp.sqrt(jnp.mean(lagged * lagged, axis=1, keepdims=True) + 1e-06)
        traces.append(lagged * inverse_rms)
    return jnp.stack(traces)


HALF = 128
LANES = 128
SRC = STEPS * GROUPS
WINDOW = 208
EDGE = WINDOW - SAMP
FAR = 1
EARLY = 2


def turns(rows, columns):
    phase = rows[:, None] * columns[None, :] % SAMP * (2.0 * math.pi / SAMP)
    pad = ((0, 0), (0, HALF - BINS)) if columns.size == BINS else ((0, HALF - BINS), (0, 0))
    return np.pad(np.cos(phase), pad), np.pad(-np.sin(phase), pad)


def dft_rows():
    return np.concatenate(turns(np.arange(WINDOW), np.arange(BINS)), axis=1)


def lag_rows():
    freqs = np.arange(BINS)
    weights = np.where((freqs == 0) | (freqs == SAMP // 2), 1.0, 2.0)
    weights = np.pad(weights, (0, HALF - BINS))[:, None]
    tables = turns(freqs, np.arange(LAGS) - LAGS // 2)
    return np.concatenate([weights * table for table in tables], axis=0)


def near_columns(n_grp, n_ch):
    return -(-(n_grp * CH_DEV + n_ch // 16 + 1) // LANES) * LANES


def window_of(seg):
    return seg * SAMP - seg % 2 * EDGE


def partial_kernel(
    n_chan,
    n_grp,
    rec_hbm,
    lengths_hbm,
    pick_hbm,
    dft_hbm,
    lag_hbm,
    out_ref,
    lengths_ref,
    pick_ref,
    rec_buf,
    dft_ref,
    lag_ref,
    send_buf,
    recv_buf,
    load_sems,
    send_sem,
    recv_sem,
):
    rows, n_ch = rec_buf.shape
    near = near_columns(n_grp, n_ch)
    segs = rows // SAMP
    n_recv = n_chan * CH_DEV
    half = n_chan // 2
    me, group = lax.axis_index("chan"), lax.axis_index("grp")
    pair, side = group // 2, group % 2
    first = (1 - side) * half
    want = jnp.where(me < half, 1, 0)
    keeps = side == want
    source_grp = pair * 2 + want

    def target(slot):
        return (first + slot // 2, pair * 2 + slot % 2)

    loads = [
        pltpu.make_async_copy(src, dst, load_sems.at[i])
        for i, (src, dst) in enumerate(
            [
                (lengths_hbm, lengths_ref),
                (pick_hbm, pick_ref),
                (rec_hbm.at[:, pl.ds(0, near)], rec_buf.at[:, pl.ds(0, near)]),
                (dft_hbm, dft_ref),
                (lag_hbm, lag_ref),
                (rec_hbm.at[:, pl.ds(near, n_ch - near)], rec_buf.at[:, pl.ds(near, n_ch - near)]),
            ]
        )
    ]
    for load in loads:
        load.start()
    small, large, rest = loads[:2], loads[2:5], loads[5]
    barrier = pltpu.get_barrier_semaphore()

    def greet(chan):
        pl.semaphore_signal(
            barrier,
            inc=1,
            device_id=(chan, source_grp),
            device_id_type=pl.DeviceIdType.MESH,
        )

    for hop in range(1, n_chan):
        greet(lax.rem(me + hop, n_chan))
    pl.when(jnp.logical_not(keeps))(lambda: greet(me))

    place = lax.broadcasted_iota(jnp.int32, (n_recv, 1), 0)
    slot_chan, slot_grp = target(place // CH_DEV)
    receivers = (slot_chan * n_grp + slot_grp) * CH_DEV + place % CH_DEV

    def gauge_of(channels, columns):
        apart = lax.broadcasted_iota(jnp.int32, (channels.shape[0], columns), 1) - channels
        return jnp.where(apart == 1, 0.5, jnp.where(apart == -1, -0.5, 0.0)).astype(jnp.bfloat16)

    recv_gauge = gauge_of(receivers, n_ch)

    for copy in small:
        copy.wait()
    line = lax.broadcasted_iota(jnp.int32, (STEPS, 128), 1)
    group_of = line % GROUPS
    lengths, picks = lengths_ref[...], pick_ref[...]
    ends = jnp.zeros((STEPS, 128), jnp.int32)
    starts, finish, spots = ends, ends, ends
    for g in range(GROUPS):
        length = jnp.broadcast_to(lengths[:, g : g + 1], ends.shape)
        pick = jnp.broadcast_to(picks[:, g : g + 1], ends.shape)
        spots = jnp.where(group_of == g, ends + lax.shift_right_logical(length * pick, 16), spots)
        starts = jnp.where(group_of == g, ends, starts)
        ends = ends + length
        finish = jnp.where(group_of == g, ends, finish)
    own_step = lax.broadcasted_iota(jnp.int32, ends.shape, 0) == line // GROUPS

    def in_line(table):
        return jnp.sum(jnp.where(own_step, table, 0), axis=0, keepdims=True)

    starts, finish = in_line(starts)[:, :SRC], in_line(finish)[:, :SRC]
    down = lax.broadcasted_iota(jnp.int32, (SRC, 128), 0)
    along = lax.broadcasted_iota(jnp.int32, (SRC, 128), 1)
    sources = jnp.where(down == along, in_line(spots).astype(jnp.float32), 0.0)
    sources = jnp.sum(sources, axis=1, keepdims=True).astype(jnp.int32)
    member = (starts <= receivers) & (receivers < finish)
    step_of = lax.broadcasted_iota(jnp.int32, (n_recv, SRC), 1) // GROUPS
    lanes = lax.broadcasted_iota(jnp.int32, (1, WINDOW), 1)

    def strain_of(gauge, seg):
        window = rec_buf[pl.ds(window_of(seg), WINDOW), pl.ds(0, gauge.shape[1])]
        return lax.dot_general(
            gauge, window, (((1,), (1,)), ((), ())), preferred_element_type=jnp.float32
        )

    def within(seg, series):
        if seg % 2 == 0:
            tail = jnp.where(lanes[:, LANES:] < SAMP, series[:, LANES:], 0.0)
            return jnp.concatenate([series[:, :LANES], tail], axis=1)
        head = jnp.where(lanes[:, :LANES] >= EDGE, series[:, :LANES], 0.0)
        return jnp.concatenate([head, series[:, LANES:]], axis=1)

    def center_of(seg, strain):
        wide = strain.astype(jnp.bfloat16).astype(jnp.float32)
        mean = jnp.sum(within(seg, wide), axis=1, keepdims=True) * (1.0 / SAMP)
        centered = within(seg, wide - mean)
        mean_square = jnp.sum(centered * centered, axis=1, keepdims=True) * (1.0 / SAMP)
        return centered.astype(jnp.bfloat16), lax.rsqrt(mean_square + 1e-06)

    def spectra_of(strains):
        parts = [center_of(seg, strain) for seg, strain in enumerate(strains)]
        series = jnp.concatenate([part[0] for part in parts], axis=0)
        spec = jnp.dot(series, dft_ref[...], preferred_element_type=jnp.float32)
        specs, count = [], strains[0].shape[0]
        for seg, (_, scale) in enumerate(parts):
            part = spec[seg * count : (seg + 1) * count]
            specs.append((part * scale).astype(jnp.bfloat16))
        return specs

    def correlate(slots, receivers, sources):
        begin, end = slots.start * CH_DEV, slots.stop * CH_DEV
        count = end - begin
        spread = jnp.concatenate(
            [jnp.where(member[begin:end] & (step_of[begin:end] == j), 1.0, 0.0) for j in range(STEPS)],
            axis=0,
        ).astype(jnp.bfloat16)
        crosses = [[0.0, 0.0] for _ in range(STEPS)]
        for receiver, source in zip(receivers, sources):
            source = jnp.dot(spread, source, preferred_element_type=jnp.float32)
            rec_real = receiver[:, :HALF].astype(jnp.float32)
            rec_imag = receiver[:, HALF:].astype(jnp.float32)
            for j in range(STEPS):
                src_real = source[j * count : (j + 1) * count, :HALF]
                src_imag = source[j * count : (j + 1) * count, HALF:]
                crosses[j][0] += src_real * rec_real + src_imag * rec_imag
                crosses[j][1] += src_real * rec_imag - src_imag * rec_real
        cross = [jnp.concatenate(parts, axis=1).astype(jnp.bfloat16) for parts in crosses]
        lagged = jnp.dot(
            jnp.concatenate(cross, axis=0), lag_ref[...], preferred_element_type=jnp.float32
        ).astype(jnp.bfloat16)
        return [
            lagged[j * count : (j + 1) * count].reshape(len(slots), CH_DEV, LAGS)
            for j in range(STEPS)
        ]

    own = jnp.where(keeps, 2 * (me - first) + side, n_chan)
    far = jnp.where(me < n_chan - FAR, 0, 1)

    def send(slot):
        return pltpu.make_async_remote_copy(
            src_ref=send_buf.at[slot],
            dst_ref=recv_buf.at[me],
            send_sem=send_sem,
            recv_sem=recv_sem.at[far],
            device_id=target(slot),
            device_id_type=pl.DeviceIdType.MESH,
        )

    def hand_out(slots):
        for slot in slots:
            pl.when(own != slot)(lambda: send(slot).start())
        pl.when((own >= slots.start) & (own < slots.stop))(
            lambda: pltpu.make_async_copy(send_buf.at[own], recv_buf.at[me], recv_sem.at[far]).start()
        )

    early, late = range(EARLY), range(EARLY, n_chan)
    split = EARLY * CH_DEV
    for load in large:
        load.wait()

    def go_early():
        front = jnp.concatenate(
            [recv_gauge[:split, :near], gauge_of(sources, near)], axis=0
        )
        specs = spectra_of([strain_of(front, seg) for seg in range(segs)])
        blocks = correlate(early, [spec[:split] for spec in specs], [spec[split:] for spec in specs])
        for j, block in enumerate(blocks):
            send_buf[pl.ds(0, EARLY), j] = block
        enter()
        hand_out(early)

    def enter():
        pl.semaphore_wait(barrier, jnp.where(keeps, n_chan - 1, n_chan))

    def finish_with(slots):
        rest.wait()
        skip = slots.start * CH_DEV
        whole = jnp.concatenate([recv_gauge[skip:], gauge_of(sources, n_ch)], axis=0)
        specs = spectra_of([strain_of(whole, seg) for seg in range(segs)])
        held = n_recv - skip
        blocks = correlate(slots, [spec[:held] for spec in specs], [spec[held:] for spec in specs])
        for j, block in enumerate(blocks):
            send_buf[pl.ds(slots.start, len(slots)), j] = block

    @pl.when(side == 1)
    def _():
        go_early()
        finish_with(late)
        hand_out(late)

    @pl.when(side == 0)
    def _():
        finish_with(range(n_chan))
        enter()
        hand_out(range(n_chan))

    def finish_sends():
        most = send_buf.at[pl.ds(0, n_chan - 1)]
        pltpu.make_async_copy(most, most, send_sem).wait()
        pl.when(jnp.logical_not(keeps))(
            lambda: pltpu.make_async_copy(send_buf.at[0], send_buf.at[0], send_sem).wait()
        )

    total = 0.0
    for k, chans in enumerate((pl.ds(0, n_chan - FAR), pl.ds(n_chan - FAR, FAR))):
        if k == 1:
            finish_sends()
        blocks = recv_buf.at[chans]
        pltpu.make_async_copy(blocks, blocks, recv_sem.at[k]).wait()
        total += jnp.sum(blocks[...].astype(jnp.float32), axis=0)
    mean_square = jnp.sum(total * total, axis=-1, keepdims=True) * (1.0 / LAGS)
    out_ref[...] = total * lax.rsqrt(mean_square + 1e-06)


def segment_shards(n_chan, n_grp, record, group_lengths, source_pick):
    rows, n_ch = record.shape
    dft = jnp.asarray(dft_rows(), jnp.bfloat16)
    lag = jnp.asarray(lag_rows(), jnp.bfloat16)
    operands = (record, group_lengths, source_pick, dft, lag)
    block = (STEPS, CH_DEV, LAGS)
    return pl.pallas_call(
        functools.partial(partial_kernel, n_chan, n_grp),
        out_shape=jax.ShapeDtypeStruct(block, jnp.float32),
        in_specs=[pl.BlockSpec(memory_space=pltpu.HBM)] * 5,
        out_specs=pl.BlockSpec(memory_space=pltpu.VMEM),
        scratch_shapes=[
            pltpu.VMEM((STEPS, GROUPS), jnp.int32),
            pltpu.VMEM((STEPS, GROUPS), jnp.int32),
            pltpu.VMEM((rows, n_ch), jnp.bfloat16),
            pltpu.VMEM(dft.shape, jnp.bfloat16),
            pltpu.VMEM(lag.shape, jnp.bfloat16),
            pltpu.VMEM((n_chan,) + block, jnp.bfloat16),
            pltpu.VMEM((n_chan,) + block, jnp.bfloat16),
            pltpu.SemaphoreType.DMA((6,)),
            pltpu.SemaphoreType.DMA,
            pltpu.SemaphoreType.DMA((2,)),
        ],
        compiler_params=pltpu.CompilerParams(
            collective_id=0, has_side_effects=True, vmem_limit_bytes=32 * 1024 * 1024
        ),
    )(*(pltpu.with_memory_space_constraint(x, pltpu.HBM) for x in operands))


def solution(mesh):
    n_chan, n_grp = mesh.shape["chan"], mesh.shape["grp"]

    def local(record, group_lengths, source_pick):
        rows, n_ch = record.shape
        wide = near_columns(n_grp, n_ch) < n_ch
        if rows % (2 * SAMP) == 0 and n_chan * CH_DEV % 128 == 0 and n_grp % 2 == 0 and wide:
            return segment_shards(n_chan, n_grp, record, group_lengths, source_pick)
        return shards(record, group_lengths, source_pick)

    return jax.shard_map(
        local,
        mesh=mesh,
        in_specs=(P("chan", None), P(), P()),
        out_specs=P(None, ("chan", "grp"), None),
        check_vma=False,
    )
```
